256 devices in a mesh: seg: 64 (over z, x, core), head: 4 (over y).
Axes of the slice: x: 4, y: 4, z: 8, core: 2. Of those that a mesh axis runs over, the one named last changes fastest.
Arguments:
- queries: bfloat16 [16384, 1536], P(('seg', 'head')), may hold values from -8 to 8
- key_rows: bfloat16 [16384, 1536], P(('seg', 'head')), may hold values from -8 to 8
- value_rows: bfloat16 [16384, 1536], P(('seg', 'head')), may hold values from -6 to 6
- w_first: float32 [24, 64, 256], P('head'), may hold values from -0.75 to 0.75
- w_second: float32 [24, 256, 64], P('head'), may hold values from -0.375 to 0.375
- gate_pairs: float32 [2, 1536], P(None, 'head'), may hold values from 0.3 to 1.5
Outputs:
- mixed: float32 [16384, 1536], P('seg', 'head')
The draws below stay inside these ranges and needn't reach their ends.
All inputs are finite; a program needn't handle non-finite values.
Results may differ from the reference program's by a relative error of at most 0.0011.
Values may be sent and summed in bfloat16 or wider, within the bound.
A program may use at most 128 MiB of HBM per device.

```python
import jax
import jax.numpy as jnp
from jax import lax

HEADS = 24
HEAD_DIM = 64
INNER = 256
SEG = 2048
PART = 256
TOKENS = 16384


def drawn_pair(key):
    row_count = TOKENS
    col_count = HEADS * HEAD_DIM
    base_query = jax.random.truncated_normal(jax.random.fold_in(key, 11), -4.0, 4.0, (row_count, col_count), jnp.float32)
    base_key = jax.random.truncated_normal(jax.random.fold_in(key, 12), -4.0, 4.0, (row_count, col_count), jnp.float32)
    return (base_query, base_key)


def draw_queries(key, part):
    return drawn_pair(key)[0].astype(jnp.bfloat16)


def draw_key_rows(key, part):
    return drawn_pair(key)[1].astype(jnp.bfloat16)


def block_levels(stream_key, extent, pieces, low, largest):
    def one(position, parts):
        heights = jax.random.uniform(jax.random.fold_in(jax.random.fold_in(stream_key, 6), position), (parts,), jnp.float32, low / len(pieces), largest / len(pieces))
        return jnp.repeat(jnp.exp(heights), extent[position] // parts).reshape((-1,) + (1,) * (len(extent) - position - 1))

    gain = one(*pieces[0])
    for cut in pieces[1:]:
        gain = gain * one(*cut)
    return gain


def bell_draw(stream_key, dims, deviation, bound, pieces=(), held_as=jnp.bfloat16):
    drawn = jax.random.normal(stream_key, dims, jnp.float32) * deviation
    if len(pieces) > 0:
        drawn = block_levels(stream_key, dims, pieces, -0.22, 0.18) * drawn
    return jnp.clip(drawn, min=-bound, max=bound).astype(held_as)


def setup_inputs(seed: int = 0) -> dict:
    seeds = jax.random.split(jax.random.key(seed), 7)
    queries = draw_queries(jax.random.fold_in(seeds[6], 71), 0)
    key_rows = draw_key_rows(jax.random.fold_in(seeds[6], 71), 0)
    value_rows = bell_draw(seeds[2], (TOKENS, HEADS * HEAD_DIM), 1.0, 6.0, ((0, 256),))
    w_first = bell_draw(seeds[3], (HEADS, HEAD_DIM, INNER), HEAD_DIM ** -0.5, 0.75, ((0, 4),), jnp.float32)
    w_second = bell_draw(seeds[4], (HEADS, INNER, HEAD_DIM), INNER ** -0.5, 0.375, ((0, 4),), jnp.float32)
    gate_pairs = jnp.clip(0.3 + 1.2 * jax.random.uniform(seeds[5], (2, HEADS * HEAD_DIM), jnp.float32) ** block_levels(seeds[5], (2, HEADS * HEAD_DIM), ((1, 4),), -0.2, 0.2), 0.3, 1.5)
    return dict(queries=queries, key_rows=key_rows, value_rows=value_rows, w_first=w_first, w_second=w_second, gate_pairs=gate_pairs)


inner_rate = 0.05
norm_epsilon = 1e-05
highest = lax.Precision.HIGHEST

def inner_model(inputs, first, second):
    hidden = jnp.einsum('nhd,hdf->nhf', inputs, first, precision=highest)
    mapped = jnp.einsum('nhf,hfd->nhd', jax.nn.gelu(hidden), second, precision=highest)
    centre = mapped - lax.optimization_barrier(jnp.mean(mapped, axis=-1, keepdims=True))
    spread = lax.optimization_barrier(jnp.mean(centre * centre, axis=-1, keepdims=True))
    return centre * lax.rsqrt(spread + norm_epsilon)

def inner_loss(first, second, inputs, target):
    error = inner_model(inputs, first, second) - target
    return 0.5 * jnp.sum(error * error) / inputs.shape[0]

def segment_attention(query_rows, key_block, value_block):
    head_count = query_rows.shape[1] // HEAD_DIM

    def head_step(head_index, result):
        start = head_index * HEAD_DIM
        head_query = lax.dynamic_slice_in_dim(query_rows, start, HEAD_DIM, 1)
        head_key = lax.dynamic_slice_in_dim(key_block, start, HEAD_DIM, 1)
        head_value = lax.dynamic_slice_in_dim(value_block, start, HEAD_DIM, 1)
        scores = lax.dot_general(head_query, head_key, (((1,), (1,)), ((), ())), preferred_element_type=jnp.float32) * HEAD_DIM ** (-0.5)
        scores = scores - lax.optimization_barrier(jnp.max(scores, axis=-1, keepdims=True))
        expon = jnp.exp(scores)
        weights = (expon / lax.optimization_barrier(jnp.sum(expon, axis=-1, keepdims=True))).astype(jnp.bfloat16)
        attended = jnp.dot(weights, head_value, preferred_element_type=jnp.float32)
        return lax.dynamic_update_slice_in_dim(result, attended, start, 1)
    return lax.fori_loop(0, head_count, head_step, jnp.zeros(query_rows.shape, jnp.float32))

def reference(queries, key_rows, value_rows, w_first, w_second, gate_pairs):
    token_count, width = queries.shape
    block_count = token_count // PART
    segment_count = token_count // SEG

    def one_segment(index):
        start = (index * SEG).astype(jnp.int32)
        return segment_attention(lax.dynamic_slice_in_dim(queries, start, SEG, 0), lax.dynamic_slice_in_dim(key_rows, start, SEG, 0), lax.dynamic_slice_in_dim(value_rows, start, SEG, 0))
    attention = lax.map(one_segment, jnp.arange(segment_count, dtype=jnp.int32)).reshape(token_count, width)

    def block_rows(array, index):
        start = (index * PART).astype(jnp.int32)
        return lax.dynamic_slice_in_dim(array, start, PART, 0).astype(jnp.float32).reshape(PART, HEADS, HEAD_DIM)

    def block_grad(index):
        inputs = block_rows(key_rows, index)
        target = block_rows(value_rows, index) - inputs
        return jax.grad(inner_loss, argnums=(0, 1))(w_first, w_second, inputs, target)
    grad_first, grad_second = lax.map(block_grad, jnp.arange(block_count, dtype=jnp.int32))
    ahead_first = jnp.cumsum(grad_first, axis=0)
    ahead_second = jnp.cumsum(grad_second, axis=0)
    behind_first = jnp.flip(jnp.cumsum(jnp.flip(grad_first, 0), axis=0), 0)
    behind_second = jnp.flip(jnp.cumsum(jnp.flip(grad_second, 0), axis=0), 0)
    gate_forward = jnp.tanh(gate_pairs[0])
    gate_backward = jnp.tanh(gate_pairs[1])

    def block_out(operands):
        index, af_first, af_second, bh_first, bh_second, attended = operands
        inputs = block_rows(queries, index)
        forward_out = inputs + inner_model(inputs, w_first - inner_rate * af_first, w_second - inner_rate * af_second)
        backward_out = inputs + inner_model(inputs, w_first - inner_rate * bh_first, w_second - inner_rate * bh_second)
        return attended + gate_forward * forward_out.reshape(PART, width) + gate_backward * backward_out.reshape(PART, width)
    mixed = lax.map(block_out, (jnp.arange(block_count, dtype=jnp.int32), ahead_first, ahead_second, behind_first, behind_second, attention.reshape(block_count, PART, width)))
    return mixed.reshape(token_count, width)
```

```python
import jax
import jax.numpy as jnp
from jax import lax
from jax.experimental import pallas as pl
from jax.experimental.pallas import tpu as pltpu
from jax.sharding import PartitionSpec as P

MESH = pl.DeviceIdType.MESH
F32 = jnp.float32
BF16 = jnp.bfloat16

NX, NC, NY, NZ = 4, 2, 4, 8
HEADS = 6
PAIRS = 3
ROWS = 256
WIDTH = 384
HALF = 384
PIECE = HALF // NX
RATE = 0.05
EPS = 1e-5
SCALE = 0.125 * 1.4426950408889634

CHIP_T = BF16
PLANE_T = BF16
BACK_T = F32


def nn(a, b):
    return lax.dot_general(a, b, (((1,), (0,)), ((), ())), preferred_element_type=F32)


def nt(a, b):
    return lax.dot_general(a, b, (((1,), (1,)), ((), ())), preferred_element_type=F32)


def tn(a, b):
    return lax.dot_general(a, b, (((0,), (0,)), ((), ())), preferred_element_type=F32)


def split(x):
    high = x.astype(BF16)
    return high, (x - high.astype(F32)).astype(BF16)


def half_mean(x, ones):
    high, low = split(x)
    return nn(jnp.concatenate([high, low], axis=1), ones)


GELU_A = 0.7978845608028654
GELU_B = 0.044715


def put_weights(dst, index, half, value):
    high, low = split(value)
    dst[index, half * 64 : half * 64 + 64, :] = high
    dst[index, 128 + half * 64 : 128 + half * 64 + 64, :] = low


def kernel(
    q_hbm, k_hbm, v_hbm, w1_hbm, w2_hbm, gate_ref, out_ref,
    ks, vs, qb, w1, w2, w2c, w1s, w2s, act, slope, ones,
    grad, other, chip_out, chips, plane_out, planes, back_out, before, after,
    mine, cross_out, cross, scores, att,
    local_sem, load_sem, a2a_send, a2a_recv, ring_send, ring_recv, core_send, core_recv,
    g_send, g_recv, chip_send, chip_recv, plane_send, plane_recv, back_send, back_recv,
    cross_send, cross_recv,
):
    seg = lax.axis_index("seg")
    y = lax.axis_index("head")
    z = seg // 8
    s = seg % 8
    x = s // 2
    c = s % 2

    def at(zz, xx, cc, yy):
        return {"seg": zz * 8 + xx * 2 + cc, "head": yy}

    def x_peer(d):
        return at(z, (x + d) % NX, c, y)

    twin = at(z, x, 1 - c, y)

    def remote(src, dst, send, recv, device):
        return pltpu.make_async_remote_copy(
            src_ref=src, dst_ref=dst, send_sem=send, recv_sem=recv, device_id=device, device_id_type=MESH
        )

    barrier = pltpu.get_barrier_semaphore()
    peers = [at(z, x, c, (y + d) % NY) for d in range(1, NY)]
    peers += [x_peer(d) for d in range(1, NX)]
    peers += [at((z + d) % NZ, x, c, y) for d in range(1, NZ)]
    peers += [twin]
    for peer in peers:
        pl.semaphore_signal(barrier, inc=1, device_id=peer, device_id_type=MESH)

    load1 = pltpu.make_async_copy(w1_hbm, w1, load_sem.at[0])
    load2 = pltpu.make_async_copy(w2_hbm, w2, load_sem.at[1])
    load1.start()
    load2.start()

    def part(yy):
        return pl.ds(pl.multiple_of(yy * WIDTH, 128), WIDTH)

    rows_of_y = pl.ds(pl.multiple_of(y * 64, 64), 64)
    sources = [k_hbm, v_hbm, q_hbm]
    targets = [ks.at[s, rows_of_y], vs.at[s, rows_of_y], qb.at[rows_of_y]]
    locals_ = []
    for t in range(3):
        copy = pltpu.make_async_copy(sources[t].at[:, part(y)], targets[t], local_sem.at[t])
        copy.start()
        locals_.append(copy)

    pl.semaphore_wait(barrier, len(peers))

    a2a = [[], [], []]
    for t in range(3):
        for d in range(1, NY):
            yy = (y + d) % NY
            copy = remote(
                sources[t].at[:, part(yy)], targets[t], a2a_send.at[t, d], a2a_recv.at[t, d], at(z, x, c, yy)
            )
            copy.start()
            a2a[t].append(copy)

    w1s[...] = jnp.zeros_like(w1s)
    w2s[...] = jnp.zeros_like(w2s)
    row = lax.broadcasted_iota(jnp.int32, (256, 128), 0)
    col = lax.broadcasted_iota(jnp.int32, (256, 128), 1)
    ones[...] = jnp.where((row % 128) // 64 == col // 64, 1.0 / 64, 0.0).astype(BF16)
    load1.wait()
    load2.wait()
    for h in range(HEADS):
        put_weights(w1s, h, h % 2, w1[h])
        flipped = w2[h].T
        flipped = flipped - jnp.mean(flipped, axis=0, keepdims=True)
        w2c[h] = flipped
        put_weights(w2s, h, h % 2, flipped)

    for t in range(2):
        locals_[t].wait()
        for copy in a2a[t]:
            copy.wait()

    kv = (ks, vs)
    first = []
    for t in range(2):
        for j, d in enumerate((1, NX - 1)):
            copy = remote(kv[t].at[s], kv[t].at[s], ring_send.at[t, j], ring_recv.at[t, j], x_peer(d))
            copy.start()
            first.append(copy)
    to_twin = []

    def give(t, slot, k):
        copy = remote(kv[t].at[slot], kv[t].at[slot], core_send.at[t, k], core_recv.at[t, k], twin)
        copy.start()
        to_twin.append(copy)

    for t in range(2):
        give(t, s, 0)

    def grad_pair(p, carry):
        lanes = pl.ds(pl.multiple_of(p * 128, 128), 128)
        keys = ks[s, :, lanes]
        doubled = jnp.concatenate([keys, keys], axis=1)
        centre = jnp.zeros((ROWS, 128), F32)
        for half in range(2):
            h = 2 * p + half
            hidden = nn(doubled, w1s[h])
            square = hidden * hidden
            bent = jnp.tanh(hidden * (GELU_A + GELU_A * GELU_B * square))
            rise = 0.5 + 0.5 * bent
            act[half] = (hidden * rise).astype(BF16)
            slope[half] = rise + 0.5 * hidden * (1.0 - bent * bent) * (GELU_A + 3 * GELU_A * GELU_B * square)
            u = nt(act[half], w2s[h])
            centre = centre + u[:, :128] + u[:, 128:]
        inverse = lax.rsqrt(half_mean(centre * centre, ones[...]) + EPS)
        normal = centre * inverse
        target = vs[s, :, lanes].astype(F32) - keys.astype(F32)
        error = (normal - target) * (1.0 / ROWS)
        du = inverse * (error - half_mean(error, ones[...]) - normal * half_mean(error * normal, ones[...]))
        high, low = split(du)
        both = jnp.concatenate([high, low], axis=1)
        twice = jnp.concatenate([high, high], axis=1)
        for half in range(2):
            h = 2 * p + half
            base = pl.multiple_of(p * 256 + half * 128, 128)
            second = tn(both, act[half])
            second = second[half * 64 : half * 64 + 64] + second[128 + half * 64 : 128 + half * 64 + 64]
            dh = (nn(twice, w2s[h]) * slope[half]).astype(BF16)
            grad[pl.ds(base, 64), :] = tn(keys, dh)[half * 64 : half * 64 + 64]
            grad[pl.ds(base + 64, 64), :] = second
        return carry

    lax.fori_loop(0, PAIRS, grad_pair, 0)

    own_half = pl.ds(pl.multiple_of(c * HALF, HALF), HALF)
    twin_half = pl.ds(pl.multiple_of((1 - c) * HALF, HALF), HALF)
    g_copy = remote(grad.at[twin_half], other, g_send, g_recv, twin)
    g_copy.start()
    g_copy.wait()
    chip_out[...] = (grad[own_half] + other[...]).astype(CHIP_T).reshape(NX, PIECE, 256)
    chip_copies = []
    for d in range(1, NX):
        copy = remote(chip_out.at[(x + d) % NX], chips.at[x], chip_send.at[d], chip_recv.at[d], x_peer(d))
        copy.start()
        chip_copies.append(copy)
    chips[x] = chip_out[x]

    for copy in first:
        copy.wait()
    left, right = (s + 6) % 8, (s + 2) % 8
    second_hop = []
    for t, (slot, d) in enumerate(((left, 1), (right, NX - 1))):
        copy = remote(kv[t].at[slot], kv[t].at[slot], ring_send.at[t, 2], ring_recv.at[t, 2], x_peer(d))
        copy.start()
        second_hop.append(copy)
    for t in range(2):
        give(t, left, 1)
        give(t, right, 2)

    for copy in chip_copies:
        copy.wait()
    plane = chips[0].astype(F32)
    for k in range(1, NX):
        plane = plane + chips[k].astype(F32)
    plane_out[...] = plane.astype(PLANE_T)
    plane_copies = []
    for d in (4, 3, 5, 2, 6, 1, 7):
        copy = remote(plane_out, planes.at[z], plane_send.at[d], plane_recv.at[d], at((z + d) % NZ, x, c, y))
        copy.start()
        plane_copies.append(copy)

    for copy in second_hop:
        copy.wait()
    for t in range(2):
        give(t, (s + 4) % 8, 3)
    locals_[2].wait()
    for copy in a2a[2]:
        copy.wait()
    for copy in to_twin:
        copy.wait()

    lane = lax.broadcasted_iota(jnp.int32, (ROWS, 128), 1)

    def attend(p, carry):
        lanes = pl.ds(pl.multiple_of(p * 128, 128), 128)
        pair = qb[:, lanes]
        result = []
        for half in range(2):
            query = jnp.where(lane // 64 == half, pair, jnp.zeros_like(pair))
            top = None
            for j in range(8):
                block = nt(query, ks[j, :, lanes])
                scores[j] = block
                peak = jnp.maximum(block[:, :128], block[:, 128:])
                top = peak if top is None else jnp.maximum(top, peak)
            top = jnp.max(top, axis=1, keepdims=True)
            total = jnp.zeros((ROWS, 128), F32)
            summed = jnp.zeros((ROWS, 128), F32)
            for j in range(8):
                weight = jnp.exp2((scores[j] - top) * SCALE)
                total = total + weight[:, :128] + weight[:, 128:]
                summed = summed + nn(weight.astype(BF16), vs[j, :, lanes])
            result.append(summed / jnp.sum(total, axis=1, keepdims=True))
        att[:, lanes] = jnp.where(lane < 64, result[0], result[1])
        return carry

    lax.fori_loop(0, 1, attend, 0)

    for copy in plane_copies:
        copy.wait()
    low_sum = jnp.zeros((PIECE, 256), F32)
    high_sum = jnp.zeros((PIECE, 256), F32)
    for d in range(1, NZ):
        zz = (z + d) % NZ
        value = planes[zz].astype(F32)
        low_sum = low_sum + jnp.where(zz < z, value, 0.0)
        high_sum = high_sum + jnp.where(zz > z, value, 0.0)
    ahead_of = []
    run = low_sum
    for k in range(NX):
        ahead_of.append(run)
        run = run + chips[k].astype(F32)
    run = high_sum
    for k in reversed(range(NX)):
        back_out[k, 0] = ahead_of[k].astype(BACK_T)
        back_out[k, 1] = run.astype(BACK_T)
        run = run + chips[k].astype(F32)
    rows_of_x = pl.ds(pl.multiple_of(x * PIECE, PIECE), PIECE)
    back_copies = []
    for d in (2, 1, 3):
        for side, dst in enumerate((before, after)):
            copy = remote(
                back_out.at[(x + d) % NX, side], dst.at[rows_of_x], back_send.at[side, d], back_recv.at[side, d],
                x_peer(d),
            )
            copy.start()
            back_copies.append(copy)
    before[rows_of_x] = back_out[x, 0]
    after[rows_of_x] = back_out[x, 1]

    lax.fori_loop(1, PAIRS, attend, 0)

    for copy in back_copies:
        copy.wait()
    is_one = c.astype(F32)
    is_zero = 1.0 - is_one
    own = grad[own_half]
    oth = other[...]
    cross_out[0] = before[...].astype(F32) + oth + is_zero * own
    cross_out[1] = after[...].astype(F32) + oth + is_one * own
    cross_copies = []
    for side in range(2):
        copy = remote(cross_out.at[side], cross.at[side], cross_send.at[side], cross_recv.at[side], twin)
        copy.start()
        cross_copies.append(copy)
    mine[0] = before[...].astype(F32) + own + is_one * oth
    mine[1] = after[...].astype(F32) + own + is_zero * oth
    for copy in cross_copies:
        copy.wait()
    for side in range(2):
        for h in range(HEADS):
            k = h % 3
            is_own = c if h >= 3 else 1 - c
            sl = slice(k * 128, k * 128 + 64)
            sr = slice(k * 128 + 64, k * 128 + 128)
            keep = is_own > 0
            put_weights(w1s, h, h % 2, w1[h] - RATE * jnp.where(keep, mine[side, sl], cross[side, sl]))
            put_weights(w2s, h, h % 2, w2c[h] - RATE * jnp.where(keep, mine[side, sr], cross[side, sr]))

        def final_pair(p, carry):
            lanes = pl.ds(pl.multiple_of(p * 128, 128), 128)
            query = qb[:, lanes]
            doubled = jnp.concatenate([query, query], axis=1)
            centre = jnp.zeros((ROWS, 128), F32)
            for half in range(2):
                h = 2 * p + half
                hidden = nn(doubled, w1s[h])
                bent = jnp.tanh(hidden * (GELU_A + GELU_A * GELU_B * hidden * hidden))
                high, low = split(hidden * (0.5 + 0.5 * bent))
                u = nt(high, w2s[h])
                centre = centre + u[:, :128] + u[:, 128:] + nt(low, w2s[h, :128, :])
            inverse = lax.rsqrt(half_mean(centre * centre, ones[...]) + EPS)
            gate = jnp.tanh(gate_ref[side : side + 1, lanes])
            att[:, lanes] = att[:, lanes] + gate * (query.astype(F32) + centre * inverse)
            return carry

        lax.fori_loop(0, PAIRS, final_pair, 0)
    out_ref[...] = att[...]


def on_device(queries, key_rows, value_rows, w_first, w_second, gate_pairs):
    dma = pltpu.SemaphoreType.DMA
    hbm = pl.BlockSpec(memory_space=pl.ANY)
    vmem = pl.BlockSpec(memory_space=pltpu.VMEM)
    scratch = [
        pltpu.VMEM((8, ROWS, WIDTH), BF16),
        pltpu.VMEM((8, ROWS, WIDTH), BF16),
        pltpu.VMEM((ROWS, WIDTH), BF16),
        pltpu.VMEM((HEADS, 64, 256), F32),
        pltpu.VMEM((HEADS, 256, 64), F32),
        pltpu.VMEM((HEADS, 64, 256), F32),
        pltpu.VMEM((HEADS, 256, 256), BF16),
        pltpu.VMEM((HEADS, 256, 256), BF16),
        pltpu.VMEM((2, ROWS, 256), BF16),
        pltpu.VMEM((2, ROWS, 256), F32),
        pltpu.VMEM((256, 128), BF16),
        pltpu.VMEM((2 * HALF, 256), F32),
        pltpu.VMEM((HALF, 256), F32),
        pltpu.VMEM((NX, PIECE, 256), CHIP_T),
        pltpu.VMEM((NX, PIECE, 256), CHIP_T),
        pltpu.VMEM((PIECE, 256), PLANE_T),
        pltpu.VMEM((NZ, PIECE, 256), PLANE_T),
        pltpu.VMEM((NX, 2, PIECE, 256), BACK_T),
        pltpu.VMEM((HALF, 256), BACK_T),
        pltpu.VMEM((HALF, 256), BACK_T),
        pltpu.VMEM((2, HALF, 256), F32),
        pltpu.VMEM((2, HALF, 256), F32),
        pltpu.VMEM((2, HALF, 256), F32),
        pltpu.VMEM((8, ROWS, 256), F32),
        pltpu.VMEM((ROWS, WIDTH), F32),
        dma((3,)),
        dma((2,)),
        dma((3, NY)),
        dma((3, NY)),
        dma((2, 3)),
        dma((2, 3)),
        dma((2, 4)),
        dma((2, 4)),
        dma,
        dma,
        dma((NX,)),
        dma((NX,)),
        dma((NZ,)),
        dma((NZ,)),
        dma((2, NX)),
        dma((2, NX)),
        dma((2,)),
        dma((2,)),
    ]
    return pl.pallas_call(
        kernel,
        out_shape=jax.ShapeDtypeStruct((ROWS, WIDTH), F32),
        in_specs=[hbm, hbm, hbm, hbm, hbm, vmem],
        out_specs=vmem,
        scratch_shapes=scratch,
        compiler_params=pltpu.CompilerParams(
            collective_id=0, has_side_effects=True, vmem_limit_bytes=48 * 1024 * 1024
        ),
        name="layer",
    )(queries, key_rows, value_rows, w_first, w_second, gate_pairs)


def solution(mesh):
    in_specs = (
        P(("seg", "head"), None),
        P(("seg", "head"), None),
        P(("seg", "head"), None),
        P("head", None, None),
        P("head", None, None),
        P(None, "head"),
    )
    out_specs = P("seg", "head")
    return jax.shard_map(on_device, mesh=mesh, in_specs=in_specs, out_specs=out_specs, check_vma=False)
```

```python
import jax
import jax.numpy as jnp
from jax import lax
from jax.experimental import pallas as pl
from jax.experimental.pallas import tpu as pltpu
from jax.sharding import PartitionSpec as P

MESH = pl.DeviceIdType.MESH
F32 = jnp.float32
BF16 = jnp.bfloat16

NX, NC, NY, NZ = 4, 2, 4, 8
HEADS = 6
PAIRS = 3
ROWS = 256
WIDTH = 384
BLOCK = 128
PIECE = BLOCK // NX
RATE = 0.05
EPS = 1e-5
SCALE = 0.125 * 1.4426950408889634

CHIP_T = BF16
PLANE_T = BF16
BACK_T = F32


def nn(a, b):
    return lax.dot_general(a, b, (((1,), (0,)), ((), ())), preferred_element_type=F32)


def nt(a, b):
    return lax.dot_general(a, b, (((1,), (1,)), ((), ())), preferred_element_type=F32)


def tn(a, b):
    return lax.dot_general(a, b, (((0,), (0,)), ((), ())), preferred_element_type=F32)


def split(x):
    high = x.astype(BF16)
    return high, (x - high.astype(F32)).astype(BF16)


def half_mean(x, ones):
    high, low = split(x)
    return nn(jnp.concatenate([high, low], axis=1), ones)


GELU_A = 0.7978845608028654
GELU_B = 0.044715


def put_weights(dst, rows, value):
    high, low = split(value)
    dst[pl.ds(rows, 64), :] = high
    dst[pl.ds(rows + 128, 64), :] = low


def kernel(
    q_hbm, k_hbm, v_hbm, w1_hbm, w2_hbm, gate_ref, out_ref,
    kv, qb, w1, w2, w2c, w1s, w2s, act, slope, ones,
    grad, other, chip_out, chips, plane_out, planes, back_out, back,
    cross_out, cross, centres, scores, att,
    local_sem, load_sem, a2a_send, a2a_recv, q_send, q_recv, ring_send, ring_recv, core_send, core_recv,
    g_send, g_recv, chip_send, chip_recv, plane_send, plane_recv, back_send, back_recv,
    cross_send, cross_recv,
):
    seg = lax.axis_index("seg")
    y = lax.axis_index("head")
    z = seg // 8
    s = seg % 8
    x = s // 2
    c = s % 2

    def at(zz, xx, cc, yy):
        return {"seg": zz * 8 + xx * 2 + cc, "head": yy}

    def x_peer(d):
        return at(z, (x + d) % NX, c, y)

    twin = at(z, x, 1 - c, y)

    def send(src, dst, send_sem, recv_sem, device):
        copy = pltpu.make_async_remote_copy(
            src_ref=src, dst_ref=dst, send_sem=send_sem, recv_sem=recv_sem, device_id=device, device_id_type=MESH
        )
        copy.start()
        return copy

    def wait(copies):
        for copy in copies:
            copy.wait()

    barrier = pltpu.get_barrier_semaphore()
    peers = [at((z + d) % NZ, x, c, y) for d in range(1, NZ)]
    peers += [at(z, x, c, (y + d) % NY) for d in range(1, NY)]
    peers += [x_peer(d) for d in range(1, NX)]
    peers += [twin]
    for peer in peers:
        pl.semaphore_signal(barrier, inc=1, device_id=peer, device_id_type=MESH)

    load1 = pltpu.make_async_copy(w1_hbm, w1, load_sem.at[0])
    load2 = pltpu.make_async_copy(w2_hbm, w2, load_sem.at[1])
    load1.start()
    load2.start()

    def part(yy, p):
        return pl.ds(pl.multiple_of(yy * WIDTH + p * 128, 128), 128)

    rows_of_y = pl.ds(pl.multiple_of(y * 64, 64), 64)
    sources = (k_hbm, v_hbm)
    own_tokens = [[], [], []]
    for p in range(PAIRS):
        for t in range(2):
            copy = pltpu.make_async_copy(
                sources[t].at[:, part(y, p)], kv.at[p, s, t, rows_of_y], local_sem.at[p, t]
            )
            copy.start()
            own_tokens[p].append(copy)
    own_query = []
    for p in range(PAIRS):
        copy = pltpu.make_async_copy(q_hbm.at[:, part(y, p)], qb.at[p, rows_of_y], local_sem.at[p, 2])
        copy.start()
        own_query.append(copy)

    w1s[...] = jnp.zeros_like(w1s)
    w2s[...] = jnp.zeros_like(w2s)
    row = lax.broadcasted_iota(jnp.int32, (256, 128), 0)
    col = lax.broadcasted_iota(jnp.int32, (256, 128), 1)
    ones[...] = jnp.where((row % 128) // 64 == col // 64, 1.0 / 64, 0.0).astype(BF16)
    load1.wait()
    load2.wait()
    for h in range(HEADS):
        put_weights(w1s.at[0, h], h % 2 * 64, w1[h])
        centred = w2[h] - jnp.mean(w2[h], axis=0, keepdims=True)
        w2c[h] = centred
        put_weights(w2s.at[0, h], h % 2 * 64, centred)

    pl.semaphore_wait(barrier, len(peers))

    tokens = [[], [], []]
    for p in range(PAIRS):
        for d in (2, 1, 3):
            yy = (y + d) % NY
            for t in range(2):
                tokens[p].append(
                    send(
                        sources[t].at[:, part(yy, p)], kv.at[p, s, t, rows_of_y],
                        a2a_send.at[p, t, d], a2a_recv.at[p, t, d], at(z, x, c, yy),
                    )
                )
    query_copies = []
    for p in range(PAIRS):
        for d in (2, 1, 3):
            yy = (y + d) % NY
            query_copies.append(
                send(
                    q_hbm.at[:, part(yy, p)], qb.at[p, rows_of_y], q_send.at[p, d], q_recv.at[p, d],
                    at(z, x, c, yy),
                )
            )

    def gradients(p):
        keys = kv[p, s, 0]
        doubled = jnp.concatenate([keys, keys], axis=1)
        centre = jnp.zeros((ROWS, 128), F32)
        for half in range(2):
            h = 2 * p + half
            hidden = nn(doubled, w1s[0, h])
            square = hidden * hidden
            bent = jnp.tanh(hidden * (GELU_A + GELU_A * GELU_B * square))
            rise = 0.5 + 0.5 * bent
            act[half] = (hidden * rise).astype(BF16)
            slope[half] = rise + 0.5 * hidden * (1.0 - bent * bent) * (GELU_A + 3 * GELU_A * GELU_B * square)
            u = nt(act[half], w2s[0, h])
            centre = centre + u[:, :128] + u[:, 128:]
        inverse = lax.rsqrt(half_mean(centre * centre, ones[...]) + EPS)
        normal = centre * inverse
        target = kv[p, s, 1].astype(F32) - keys.astype(F32)
        error = (normal - target) * (1.0 / ROWS)
        du = inverse * (error - half_mean(error, ones[...]) - normal * half_mean(error * normal, ones[...]))
        high, low = split(du)
        both = jnp.concatenate([high, low], axis=1)
        twice = jnp.concatenate([high, high], axis=1)
        for half in range(2):
            second = tn(both, act[half])
            second = second[half * 64 : half * 64 + 64] + second[128 + half * 64 : 128 + half * 64 + 64]
            dh = (nn(twice, w2s[0, 2 * p + half]) * slope[half]).astype(BF16)
            grad[p, half, :64] = tn(keys, dh)[half * 64 : half * 64 + 64]
            grad[p, half, 64:] = second

    def to_other_core(p):
        return send(grad.at[p, 1 - c], other.at[p], g_send.at[p], g_recv.at[p], twin)

    def along_x(p):
        chip_out[p] = (grad[p, c] + other[p]).astype(CHIP_T).reshape(NX, PIECE, 256)
        copies = [
            send(chip_out.at[p, (x + d) % NX], chips.at[p, x], chip_send.at[p, d], chip_recv.at[p, d], x_peer(d))
            for d in (2, 1, 3)
        ]
        chips[p, x] = chip_out[p, x]
        return copies

    def along_z(p):
        plane = chips[p, 0].astype(F32)
        for k in range(1, NX):
            plane = plane + chips[p, k].astype(F32)
        plane_out[p] = plane.astype(PLANE_T)
        return [
            send(
                plane_out.at[p], planes.at[p, z], plane_send.at[p, d], plane_recv.at[p, d],
                at((z + d) % NZ, x, c, y),
            )
            for d in (4, 3, 5, 2, 6, 1, 7)
        ]

    def back_along_x(p):
        low_sum = jnp.zeros((PIECE, 256), F32)
        high_sum = jnp.zeros((PIECE, 256), F32)
        for d in range(1, NZ):
            zz = (z + d) % NZ
            value = planes[p, zz].astype(F32)
            low_sum = low_sum + jnp.where(zz < z, value, 0.0)
            high_sum = high_sum + jnp.where(zz > z, value, 0.0)
        ahead_of = []
        run = low_sum
        for k in range(NX):
            ahead_of.append(run)
            run = run + chips[p, k].astype(F32)
        run = high_sum
        for k in reversed(range(NX)):
            back_out[p, k, 0] = ahead_of[k].astype(BACK_T)
            back_out[p, k, 1] = run.astype(BACK_T)
            run = run + chips[p, k].astype(F32)
        copies = [
            send(back_out.at[p, (x + d) % NX], back.at[p, x], back_send.at[p, d], back_recv.at[p, d], x_peer(d))
            for d in (2, 1, 3)
        ]
        back[p, x] = back_out[p, x]
        return copies

    is_one = c.astype(F32)
    is_zero = 1.0 - is_one

    def to_twin(p):
        own, oth = grad[p, c], other[p]
        ahead = back[p, :, 0].reshape(BLOCK, 256).astype(F32) + oth
        behind = back[p, :, 1].reshape(BLOCK, 256).astype(F32) + oth
        cross_out[p, 0] = ahead + is_zero * own
        cross_out[p, 1] = behind + is_one * own
        return [send(cross_out.at[p], cross.at[p], cross_send.at[p], cross_recv.at[p], twin)]

    def inner(p, half, side, value):
        h = 2 * p + half
        rows = pl.multiple_of(half * 64, 64)
        put_weights(w1s.at[side, h], rows, w1[h] - RATE * value[:64])
        put_weights(w2s.at[side, h], rows, w2c[h] - RATE * value[64:])
        query = qb[p]
        hidden = nn(jnp.concatenate([query, query], axis=1), w1s[side, h])
        bent = jnp.tanh(hidden * (GELU_A + GELU_A * GELU_B * hidden * hidden))
        high, low = split(hidden * (0.5 + 0.5 * bent))
        u = nt(high, w2s[side, h])
        return u[:, :128] + u[:, 128:] + nt(low, w2s[side, h, :128, :])

    def own_inner(p):
        own, oth = grad[p, c], other[p]
        ahead = back[p, :, 0].reshape(BLOCK, 256).astype(F32) + own + is_one * oth
        behind = back[p, :, 1].reshape(BLOCK, 256).astype(F32) + own + is_zero * oth
        centres[p, 0] = inner(p, c, 0, ahead)
        centres[p, 1] = inner(p, c, 1, behind)

    def finish(p):
        query = qb[p].astype(F32)
        result = att[p]
        for side in range(2):
            centre = centres[p, side] + inner(p, 1 - c, side, cross[p, side])
            inverse = lax.rsqrt(half_mean(centre * centre, ones[...]) + EPS)
            gate = jnp.tanh(gate_ref[side : side + 1, p * 128 : p * 128 + 128])
            result = result + gate * (query + centre * inverse)
        out_ref[:, p * 128 : p * 128 + 128] = result

    left, right, far = (s + 6) % 8, (s + 2) % 8, (s + 4) % 8
    given = [[], [], []]

    def give(p, slot, k):
        given[p].append(send(kv.at[p, slot], kv.at[p, slot], core_send.at[p, k], core_recv.at[p, k], twin))

    def first_hop(p):
        give(p, s, 0)
        return [
            send(kv.at[p, s], kv.at[p, s], ring_send.at[p, k], ring_recv.at[p, k], x_peer(d))
            for k, d in enumerate((1, NX - 1))
        ]

    def second_hop(p):
        copies = [
            send(kv.at[p, slot, t], kv.at[p, slot, t], ring_send.at[p, 2 + t], ring_recv.at[p, 2 + t], x_peer(d))
            for t, (slot, d) in enumerate(((left, 1), (right, NX - 1)))
        ]
        give(p, left, 1)
        give(p, right, 2)
        return copies

    lane = lax.broadcasted_iota(jnp.int32, (ROWS, 128), 1)

    def attend(p):
        pair = qb[p]

        def one(half):
            query = jnp.where(lane // 64 == half, pair, jnp.zeros_like(pair))
            top = None
            for j in range(8):
                block = nt(query, kv[p, j, 0])
                scores[j] = block
                peak = jnp.maximum(block[:, :128], block[:, 128:])
                top = peak if top is None else jnp.maximum(top, peak)
            top = jnp.max(top, axis=1, keepdims=True)
            total = jnp.zeros((ROWS, 128), F32)
            summed = jnp.zeros((ROWS, 128), F32)
            for j in range(8):
                weight = jnp.exp2((scores[j] - top) * SCALE)
                total = total + weight[:, :128] + weight[:, 128:]
                summed = summed + nn(weight.astype(BF16), kv[p, j, 1])
            return summed / jnp.sum(total, axis=1, keepdims=True)

        first = one(0)
        att[p] = jnp.where(lane < 64, first, one(1))

    wait(own_tokens[0] + tokens[0])
    hop0 = first_hop(0)
    gradients(0)
    swap0 = to_other_core(0)
    wait(own_tokens[1] + tokens[1])
    gradients(1)
    swap1 = to_other_core(1)
    swap0.wait()
    chip0 = along_x(0)
    hop1 = first_hop(1)
    wait(own_tokens[2] + tokens[2])
    gradients(2)
    swap2 = to_other_core(2)
    swap1.wait()
    chip1 = along_x(1)
    wait(chip0)
    plane0 = along_z(0)
    swap2.wait()
    chip2 = along_x(2)
    hop2 = first_hop(2)
    wait(hop0)
    more0 = second_hop(0)
    wait(chip1)
    plane1 = along_z(1)
    wait(chip2)
    plane2 = along_z(2)
    wait(hop1)
    more1 = second_hop(1)
    wait(more0)
    give(0, far, 3)
    wait(own_query + query_copies)
    wait(given[0])
    attend(0)
    wait(hop2)
    more2 = second_hop(2)
    wait(plane0)
    back0 = back_along_x(0)
    wait(more1)
    give(1, far, 3)
    wait(plane1)
    back1 = back_along_x(1)
    wait(given[1])
    attend(1)
    wait(plane2)
    back2 = back_along_x(2)
    wait(more2)
    give(2, far, 3)
    wait(back0)
    cross0 = to_twin(0)
    own_inner(0)
    wait(given[2])
    attend(2)
    wait(back1)
    cross1 = to_twin(1)
    own_inner(1)
    wait(cross0)
    finish(0)
    wait(back2)
    cross2 = to_twin(2)
    own_inner(2)
    wait(cross1)
    finish(1)
    wait(cross2)
    finish(2)


def on_device(queries, key_rows, value_rows, w_first, w_second, gate_pairs):
    dma = pltpu.SemaphoreType.DMA
    hbm = pl.BlockSpec(memory_space=pl.ANY)
    vmem = pl.BlockSpec(memory_space=pltpu.VMEM)
    scratch = [
        pltpu.VMEM((PAIRS, 8, 2, ROWS, 128), BF16),
        pltpu.VMEM((PAIRS, ROWS, 128), BF16),
        pltpu.VMEM((HEADS, 64, 256), F32),
        pltpu.VMEM((HEADS, 64, 256), F32),
        pltpu.VMEM((HEADS, 64, 256), F32),
        pltpu.VMEM((2, HEADS, 256, 256), BF16),
        pltpu.VMEM((2, HEADS, 256, 256), BF16),
        pltpu.VMEM((2, ROWS, 256), BF16),
        pltpu.VMEM((2, ROWS, 256), F32),
        pltpu.VMEM((256, 128), BF16),
        pltpu.VMEM((PAIRS, 2, BLOCK, 256), F32),
        pltpu.VMEM((PAIRS, BLOCK, 256), F32),
        pltpu.VMEM((PAIRS, NX, PIECE, 256), CHIP_T),
        pltpu.VMEM((PAIRS, NX, PIECE, 256), CHIP_T),
        pltpu.VMEM((PAIRS, PIECE, 256), PLANE_T),
        pltpu.VMEM((PAIRS, NZ, PIECE, 256), PLANE_T),
        pltpu.VMEM((PAIRS, NX, 2, PIECE, 256), BACK_T),
        pltpu.VMEM((PAIRS, NX, 2, PIECE, 256), BACK_T),
        pltpu.VMEM((PAIRS, 2, BLOCK, 256), F32),
        pltpu.VMEM((PAIRS, 2, BLOCK, 256), F32),
        pltpu.VMEM((PAIRS, 2, ROWS, 128), F32),
        pltpu.VMEM((8, ROWS, 256), F32),
        pltpu.VMEM((PAIRS, ROWS, 128), F32),
        dma((PAIRS, 3)),
        dma((2,)),
        dma((PAIRS, 2, NY)),
        dma((PAIRS, 2, NY)),
        dma((PAIRS, NY)),
        dma((PAIRS, NY)),
        dma((PAIRS, 4)),
        dma((PAIRS, 4)),
        dma((PAIRS, 4)),
        dma((PAIRS, 4)),
        dma((PAIRS,)),
        dma((PAIRS,)),
        dma((PAIRS, NX)),
        dma((PAIRS, NX)),
        dma((PAIRS, NZ)),
        dma((PAIRS, NZ)),
        dma((PAIRS, NX)),
        dma((PAIRS, NX)),
        dma((PAIRS,)),
        dma((PAIRS,)),
    ]
    return pl.pallas_call(
        kernel,
        out_shape=jax.ShapeDtypeStruct((ROWS, WIDTH), F32),
        in_specs=[hbm, hbm, hbm, hbm, hbm, vmem],
        out_specs=vmem,
        scratch_shapes=scratch,
        compiler_params=pltpu.CompilerParams(
            collective_id=0, has_side_effects=True, vmem_limit_bytes=62 * 1024 * 1024
        ),
        name="layer",
    )(queries, key_rows, value_rows, w_first, jnp.swapaxes(w_second, 1, 2), gate_pairs)


def solution(mesh):
    in_specs = (
        P(("seg", "head"), None),
        P(("seg", "head"), None),
        P(("seg", "head"), None),
        P("head", None, None),
        P("head", None, None),
        P(None, "head"),
    )
    out_specs = P("seg", "head")
    return jax.shard_map(on_device, mesh=mesh, in_specs=in_specs, out_specs=out_specs, check_vma=False)
```

```python
import jax
import jax.numpy as jnp
from jax import lax
from jax.experimental import pallas as pl
from jax.experimental.pallas import tpu as pltpu
from jax.sharding import PartitionSpec as P

MESH = pl.DeviceIdType.MESH
F32 = jnp.float32
BF16 = jnp.bfloat16

NX, NC, NY, NZ = 4, 2, 4, 8
HEADS = 6
PAIRS = 3
ROWS = 256
WIDTH = 384
BLOCK = 128
PIECE = BLOCK // NX
RATE = 0.05
EPS = 1e-5
SCALE = 0.125 * 1.4426950408889634

CHIP_T = BF16
PLANE_T = BF16


def nn(a, b):
    return lax.dot_general(a, b, (((1,), (0,)), ((), ())), preferred_element_type=F32)


def nt(a, b):
    return lax.dot_general(a, b, (((1,), (1,)), ((), ())), preferred_element_type=F32)


def tn(a, b):
    return lax.dot_general(a, b, (((0,), (0,)), ((), ())), preferred_element_type=F32)


def split(x):
    high = x.astype(BF16)
    return high, (x - high.astype(F32)).astype(BF16)


def half_mean(x, ones):
    high, low = split(x)
    return nn(jnp.concatenate([high, low], axis=1), ones)


GELU_A = 0.7978845608028654
GELU_B = 0.044715


def put_weights(dst, rows, value):
    high, low = split(value)
    dst[pl.ds(rows, 64), :] = high
    dst[pl.ds(rows + 128, 64), :] = low


def kernel(
    q_hbm, k_hbm, v_hbm, w1_hbm, w2_hbm, gate_ref, out_ref,
    kv, qb, w1, w2, w2c, w1s, w2s, act, slope, ones,
    grad, other, chip_out, chips, plane_out, planes, part_out, part_in, total_out, total_in,
    cross_out, cross, centres, scores, att, tops, totals, sums,
    local_sem, load_sem, a2a_send, a2a_recv, q_send, q_recv, ring_send, ring_recv, core_send, core_recv,
    g_send, g_recv, chip_send, chip_recv, plane_send, plane_recv, back_send, back_recv,
    cross_send, cross_recv,
):
    seg = lax.axis_index("seg")
    y = lax.axis_index("head")
    z = seg // 8
    s = seg % 8
    x = s // 2
    c = s % 2

    def at(zz, xx, cc, yy):
        return {"seg": zz * 8 + xx * 2 + cc, "head": yy}

    def x_peer(d):
        return at(z, (x + d) % NX, c, y)

    twin = at(z, x, 1 - c, y)

    def send(src, dst, send_sem, recv_sem, device):
        copy = pltpu.make_async_remote_copy(
            src_ref=src, dst_ref=dst, send_sem=send_sem, recv_sem=recv_sem, device_id=device, device_id_type=MESH
        )
        copy.start()
        return copy

    def wait(copies):
        for copy in copies:
            copy.wait()

    barrier = pltpu.get_barrier_semaphore()
    peers = [at((z + d) % NZ, x, c, y) for d in range(1, NZ)]
    peers += [at(z, x, c, (y + d) % NY) for d in range(1, NY)]
    peers += [x_peer(d) for d in range(1, NX)]
    peers += [twin]
    for peer in peers:
        pl.semaphore_signal(barrier, inc=1, device_id=peer, device_id_type=MESH)

    load1 = pltpu.make_async_copy(w1_hbm, w1, load_sem.at[0])
    load2 = pltpu.make_async_copy(w2_hbm, w2, load_sem.at[1])
    load1.start()
    load2.start()

    def part(yy, p):
        return pl.ds(pl.multiple_of(yy * WIDTH + p * 128, 128), 128)

    rows_of_y = pl.ds(pl.multiple_of(y * 64, 64), 64)
    sources = (k_hbm, v_hbm)
    own_tokens = [[], [], []]
    for p in range(PAIRS):
        for t in range(2):
            copy = pltpu.make_async_copy(
                sources[t].at[:, part(y, p)], kv.at[p, s, t, rows_of_y], local_sem.at[p, t]
            )
            copy.start()
            own_tokens[p].append(copy)
    own_query = []
    for p in range(PAIRS):
        copy = pltpu.make_async_copy(q_hbm.at[:, part(y, p)], qb.at[p, rows_of_y], local_sem.at[p, 2])
        copy.start()
        own_query.append(copy)

    w1s[...] = jnp.zeros_like(w1s)
    w2s[...] = jnp.zeros_like(w2s)
    row = lax.broadcasted_iota(jnp.int32, (256, 128), 0)
    col = lax.broadcasted_iota(jnp.int32, (256, 128), 1)
    ones[...] = jnp.where((row % 128) // 64 == col // 64, 1.0 / 64, 0.0).astype(BF16)
    load1.wait()
    load2.wait()
    for h in range(HEADS):
        put_weights(w1s.at[0, h], h % 2 * 64, w1[h])
        centred = w2[h] - jnp.mean(w2[h], axis=0, keepdims=True)
        w2c[h] = centred
        put_weights(w2s.at[0, h], h % 2 * 64, centred)

    pl.semaphore_wait(barrier, len(peers))

    tokens = [[], [], []]
    for p in range(PAIRS):
        for d in (2, 1, 3):
            yy = (y + d) % NY
            for t in range(2):
                tokens[p].append(
                    send(
                        sources[t].at[:, part(yy, p)], kv.at[p, s, t, rows_of_y],
                        a2a_send.at[p, t, d], a2a_recv.at[p, t, d], at(z, x, c, yy),
                    )
                )
    query_copies = []
    for p in range(PAIRS):
        for d in (2, 1, 3):
            yy = (y + d) % NY
            query_copies.append(
                send(
                    q_hbm.at[:, part(yy, p)], qb.at[p, rows_of_y], q_send.at[p, d], q_recv.at[p, d],
                    at(z, x, c, yy),
                )
            )

    def gradients(p):
        keys = kv[p, s, 0]
        doubled = jnp.concatenate([keys, keys], axis=1)
        centre = jnp.zeros((ROWS, 128), F32)
        for half in range(2):
            h = 2 * p + half
            hidden = nn(doubled, w1s[0, h])
            square = hidden * hidden
            bent = jnp.tanh(hidden * (GELU_A + GELU_A * GELU_B * square))
            rise = 0.5 + 0.5 * bent
            act[half] = (hidden * rise).astype(BF16)
            slope[half] = rise + 0.5 * hidden * (1.0 - bent * bent) * (GELU_A + 3 * GELU_A * GELU_B * square)
            u = nt(act[half], w2s[0, h])
            centre = centre + u[:, :128] + u[:, 128:]
        inverse = lax.rsqrt(half_mean(centre * centre, ones[...]) + EPS)
        normal = centre * inverse
        target = kv[p, s, 1].astype(F32) - keys.astype(F32)
        error = (normal - target) * (1.0 / ROWS)
        du = inverse * (error - half_mean(error, ones[...]) - normal * half_mean(error * normal, ones[...]))
        high, low = split(du)
        both = jnp.concatenate([high, low], axis=1)
        twice = jnp.concatenate([high, high], axis=1)
        for half in range(2):
            second = tn(both, act[half])
            second = second[half * 64 : half * 64 + 64] + second[128 + half * 64 : 128 + half * 64 + 64]
            dh = (nn(twice, w2s[0, 2 * p + half]) * slope[half]).astype(BF16)
            grad[p, half, :64] = tn(keys, dh)[half * 64 : half * 64 + 64]
            grad[p, half, 64:] = second

    def to_other_core(p):
        return send(grad.at[p, 1 - c], other.at[p], g_send.at[p], g_recv.at[p], twin)

    def along_x(p):
        chip_out[p] = (grad[p, c] + other[p]).astype(CHIP_T).reshape(NX, PIECE, 256)
        copies = [
            send(chip_out.at[p, (x + d) % NX], chips.at[p, x], chip_send.at[p, d], chip_recv.at[p, d], x_peer(d))
            for d in (2, 1, 3)
        ]
        chips[p, x] = chip_out[p, x]
        return copies

    def along_z(p):
        plane = chips[p, 0].astype(F32)
        for k in range(1, NX):
            plane = plane + chips[p, k].astype(F32)
        plane_out[p] = plane.astype(PLANE_T)
        return [
            send(
                plane_out.at[p], planes.at[p, z], plane_send.at[p, d], plane_recv.at[p, d],
                at((z + d) % NZ, x, c, y),
            )
            for d in (4, 3, 5, 2, 6, 1, 7)
        ]

    low_plane = z < NZ // 2

    def back_along_x(p):
        low_sum = jnp.zeros((PIECE, 256), F32)
        high_sum = jnp.zeros((PIECE, 256), F32)
        for d in range(1, NZ):
            zz = (z + d) % NZ
            value = planes[p, zz].astype(F32)
            low_sum = low_sum + jnp.where(zz < z, value, 0.0)
            high_sum = high_sum + jnp.where(zz > z, value, 0.0)
        ahead_of = []
        run = low_sum
        for k in range(NX):
            ahead_of.append(run)
            run = run + chips[p, k].astype(F32)
        total_out[p] = run + high_sum
        run = high_sum
        for k in reversed(range(NX)):
            part_out[p, k] = jnp.where(low_plane, ahead_of[k], run).astype(BF16)
            run = run + chips[p, k].astype(F32)
        copies = []
        for d in (2, 1, 3):
            to = x_peer(d)
            copies.append(
                send(part_out.at[p, (x + d) % NX], part_in.at[p, x], back_send.at[p, 0, d], back_recv.at[p, 0, d], to)
            )
            copies.append(
                send(total_out.at[p], total_in.at[p, x], back_send.at[p, 1, d], back_recv.at[p, 1, d], to)
            )
        part_in[p, x] = part_out[p, x]
        total_in[p, x] = total_out[p]
        return copies

    is_one = c.astype(F32)
    is_zero = 1.0 - is_one

    def around(p):
        near = part_in[p].reshape(BLOCK, 256).astype(F32)
        rest = total_in[p].reshape(BLOCK, 256) - chip_out[p].reshape(BLOCK, 256).astype(F32) - near
        return jnp.where(low_plane, near, rest), jnp.where(low_plane, rest, near)

    def to_twin(p):
        own, oth = grad[p, c], other[p]
        ahead, behind = around(p)
        cross_out[p, 0] = ahead + oth + is_zero * own
        cross_out[p, 1] = behind + oth + is_one * own
        return [send(cross_out.at[p], cross.at[p], cross_send.at[p], cross_recv.at[p], twin)]

    def inner(p, half, side, value):
        h = 2 * p + half
        rows = pl.multiple_of(half * 64, 64)
        put_weights(w1s.at[side, h], rows, w1[h] - RATE * value[:64])
        put_weights(w2s.at[side, h], rows, w2c[h] - RATE * value[64:])
        query = qb[p]
        hidden = nn(jnp.concatenate([query, query], axis=1), w1s[side, h])
        bent = jnp.tanh(hidden * (GELU_A + GELU_A * GELU_B * hidden * hidden))
        high, low = split(hidden * (0.5 + 0.5 * bent))
        u = nt(high, w2s[side, h])
        return u[:, :128] + u[:, 128:] + nt(low, w2s[side, h, :128, :])

    def own_inner(p):
        own, oth = grad[p, c], other[p]
        ahead, behind = around(p)
        centres[p, 0] = inner(p, c, 0, ahead + own + is_one * oth)
        centres[p, 1] = inner(p, c, 1, behind + own + is_zero * oth)

    def finish(p):
        query = qb[p].astype(F32)
        result = att[p]
        for side in range(2):
            centre = centres[p, side] + inner(p, 1 - c, side, cross[p, side])
            inverse = lax.rsqrt(half_mean(centre * centre, ones[...]) + EPS)
            gate = jnp.tanh(gate_ref[side : side + 1, p * 128 : p * 128 + 128])
            result = result + gate * (query + centre * inverse)
        out_ref[:, p * 128 : p * 128 + 128] = result

    left, right, far = (s + 6) % 8, (s + 2) % 8, (s + 4) % 8
    given = [[], [], []]

    def twin_slot(slot):
        return slot + 1 - 2 * c

    def give(p, slot, k):
        given[p].append(send(kv.at[p, slot], kv.at[p, slot], core_send.at[p, k], core_recv.at[p, k], twin))

    def first_hop(p):
        give(p, s, 0)
        return [
            send(kv.at[p, s], kv.at[p, s], ring_send.at[p, k], ring_recv.at[p, k], x_peer(d))
            for k, d in enumerate((1, NX - 1))
        ]

    def second_hop(p):
        copies = [
            send(kv.at[p, slot, t], kv.at[p, slot, t], ring_send.at[p, 2 + t], ring_recv.at[p, 2 + t], x_peer(d))
            for t, (slot, d) in enumerate(((left, 1), (right, NX - 1)))
        ]
        give(p, left, 1)
        give(p, right, 2)
        return copies

    lane = lax.broadcasted_iota(jnp.int32, (ROWS, 128), 1)

    near_slots = (s, twin_slot(s), left, twin_slot(left), right, twin_slot(right))
    far_slots = (far, twin_slot(far))

    def attend_half(p, half, slots, last):
        pair = qb[p]
        index = 2 * p + half
        query = jnp.where(lane // 64 == half, pair, jnp.zeros_like(pair))
        top = tops[index] if last else None
        for k, slot in enumerate(slots):
            block = nt(query, kv[p, slot, 0])
            scores[k] = block
            peak = jnp.maximum(block[:, :128], block[:, 128:])
            top = peak if top is None else jnp.maximum(top, peak)
        top = jnp.max(top, axis=1, keepdims=True)
        if last:
            fade = jnp.exp2((tops[index] - top) * SCALE)
            total, summed = totals[index] * fade, sums[index] * fade
        else:
            total = jnp.zeros((ROWS, 128), F32)
            summed = jnp.zeros((ROWS, 128), F32)
        for k, slot in enumerate(slots):
            weight = jnp.exp2((scores[k] - top) * SCALE)
            total = total + weight[:, :128] + weight[:, 128:]
            summed = summed + nn(weight.astype(BF16), kv[p, slot, 1])
        if last:
            summed = summed / jnp.sum(total, axis=1, keepdims=True)
            att[p] = summed if half == 0 else jnp.where(lane < 64, att[p], summed)
        else:
            tops[index] = jnp.broadcast_to(top, (ROWS, 128))
            totals[index] = total
            sums[index] = summed

    def attend_near(p, half):
        attend_half(p, half, near_slots, False)

    def attend_far(p):
        for half in range(2):
            attend_half(p, half, far_slots, True)

    wait(own_tokens[0] + tokens[0])
    hop0 = first_hop(0)
    gradients(0)
    swap0 = to_other_core(0)
    wait(own_tokens[1] + tokens[1])
    hop1 = first_hop(1)
    gradients(1)
    swap1 = to_other_core(1)
    swap0.wait()
    chip0 = along_x(0)
    wait(own_tokens[2] + tokens[2])
    hop2 = first_hop(2)
    gradients(2)
    swap2 = to_other_core(2)
    swap1.wait()
    chip1 = along_x(1)
    swap2.wait()
    chip2 = along_x(2)
    wait(hop0)
    more0 = second_hop(0)
    wait(chip0)
    plane0 = along_z(0)
    wait(chip1)
    plane1 = along_z(1)
    wait(chip2)
    plane2 = along_z(2)
    wait(own_query + query_copies)
    wait(given[0])
    attend_near(0, 0)
    attend_near(0, 1)
    wait(hop1)
    more1 = second_hop(1)
    wait(plane0)
    back0 = back_along_x(0)
    wait(hop2)
    more2 = second_hop(2)
    wait(given[1])
    attend_near(1, 0)
    wait(plane1)
    back1 = back_along_x(1)
    attend_near(1, 1)
    wait(more0)
    give(0, far, 3)
    wait(given[2])
    attend_near(2, 0)
    wait(plane2)
    back2 = back_along_x(2)
    wait(more1)
    give(1, far, 3)
    attend_near(2, 1)
    wait(more2)
    give(2, far, 3)
    wait(back0)
    cross0 = to_twin(0)
    wait(given[0][3:])
    attend_far(0)
    own_inner(0)
    wait(back1)
    cross1 = to_twin(1)
    wait(given[1][3:])
    attend_far(1)
    own_inner(1)
    wait(given[2][3:])
    attend_far(2)
    wait(cross0)
    finish(0)
    wait(back2)
    cross2 = to_twin(2)
    own_inner(2)
    wait(cross1)
    finish(1)
    wait(cross2)
    finish(2)


def on_device(queries, key_rows, value_rows, w_first, w_second, gate_pairs):
    dma = pltpu.SemaphoreType.DMA
    hbm = pl.BlockSpec(memory_space=pl.ANY)
    vmem = pl.BlockSpec(memory_space=pltpu.VMEM)
    scratch = [
        pltpu.VMEM((PAIRS, 8, 2, ROWS, 128), BF16),
        pltpu.VMEM((PAIRS, ROWS, 128), BF16),
        pltpu.VMEM((HEADS, 64, 256), F32),
        pltpu.VMEM((HEADS, 64, 256), F32),
        pltpu.VMEM((HEADS, 64, 256), F32),
        pltpu.VMEM((2, HEADS, 256, 256), BF16),
        pltpu.VMEM((2, HEADS, 256, 256), BF16),
        pltpu.VMEM((2, ROWS, 256), BF16),
        pltpu.VMEM((2, ROWS, 256), F32),
        pltpu.VMEM((256, 128), BF16),
        pltpu.VMEM((PAIRS, 2, BLOCK, 256), F32),
        pltpu.VMEM((PAIRS, BLOCK, 256), F32),
        pltpu.VMEM((PAIRS, NX, PIECE, 256), CHIP_T),
        pltpu.VMEM((PAIRS, NX, PIECE, 256), CHIP_T),
        pltpu.VMEM((PAIRS, PIECE, 256), PLANE_T),
        pltpu.VMEM((PAIRS, NZ, PIECE, 256), PLANE_T),
        pltpu.VMEM((PAIRS, NX, PIECE, 256), BF16),
        pltpu.VMEM((PAIRS, NX, PIECE, 256), BF16),
        pltpu.VMEM((PAIRS, PIECE, 256), F32),
        pltpu.VMEM((PAIRS, NX, PIECE, 256), F32),
        pltpu.VMEM((PAIRS, 2, BLOCK, 256), F32),
        pltpu.VMEM((PAIRS, 2, BLOCK, 256), F32),
        pltpu.VMEM((PAIRS, 2, ROWS, 128), F32),
        pltpu.VMEM((6, ROWS, 256), F32),
        pltpu.VMEM((PAIRS, ROWS, 128), F32),
        pltpu.VMEM((HEADS, ROWS, 128), F32),
        pltpu.VMEM((HEADS, ROWS, 128), F32),
        pltpu.VMEM((HEADS, ROWS, 128), F32),
        dma((PAIRS, 3)),
        dma((2,)),
        dma((PAIRS, 2, NY)),
        dma((PAIRS, 2, NY)),
        dma((PAIRS, NY)),
        dma((PAIRS, NY)),
        dma((PAIRS, 4)),
        dma((PAIRS, 4)),
        dma((PAIRS, 4)),
        dma((PAIRS, 4)),
        dma((PAIRS,)),
        dma((PAIRS,)),
        dma((PAIRS, NX)),
        dma((PAIRS, NX)),
        dma((PAIRS, NZ)),
        dma((PAIRS, NZ)),
        dma((PAIRS, 2, NX)),
        dma((PAIRS, 2, NX)),
        dma((PAIRS,)),
        dma((PAIRS,)),
    ]
    return pl.pallas_call(
        kernel,
        out_shape=jax.ShapeDtypeStruct((ROWS, WIDTH), F32),
        in_specs=[hbm, hbm, hbm, hbm, hbm, vmem],
        out_specs=vmem,
        scratch_shapes=scratch,
        compiler_params=pltpu.CompilerParams(
            collective_id=0, has_side_effects=True, vmem_limit_bytes=62 * 1024 * 1024
        ),
        name="layer",
    )(queries, key_rows, value_rows, w_first, jnp.swapaxes(w_second, 1, 2), gate_pairs)


def solution(mesh):
    in_specs = (
        P(("seg", "head"), None),
        P(("seg", "head"), None),
        P(("seg", "head"), None),
        P("head", None, None),
        P("head", None, None),
        P(None, "head"),
    )
    out_specs = P("seg", "head")
    return jax.shard_map(on_device, mesh=mesh, in_specs=in_specs, out_specs=out_specs, check_vma=False)
```

```python
import jax
import jax.numpy as jnp
from jax import lax
from jax.experimental import pallas as pl
from jax.experimental.pallas import tpu as pltpu
from jax.sharding import PartitionSpec as P

MESH = pl.DeviceIdType.MESH
F32 = jnp.float32
BF16 = jnp.bfloat16

NX, NC, NY, NZ = 4, 2, 4, 8
HEADS = 6
PAIRS = 3
ROWS = 256
WIDTH = 384
BLOCK = 128
PIECE = BLOCK // NX
RATE = 0.05
EPS = 1e-5
SCALE = 0.125 * 1.4426950408889634

CHIP_T = BF16
PLANE_T = BF16


def nn(a, b):
    return lax.dot_general(a, b, (((1,), (0,)), ((), ())), preferred_element_type=F32)


def nt(a, b):
    return lax.dot_general(a, b, (((1,), (1,)), ((), ())), preferred_element_type=F32)


def tn(a, b):
    return lax.dot_general(a, b, (((0,), (0,)), ((), ())), preferred_element_type=F32)


def split(x):
    high = x.astype(BF16)
    return high, (x - high.astype(F32)).astype(BF16)


def half_mean(x, ones):
    high, low = split(x)
    return nn(jnp.concatenate([high, low], axis=1), ones)


GELU_A = 0.7978845608028654
GELU_B = 0.044715


def put_weights(dst, rows, value):
    high, low = split(value)
    dst[pl.ds(rows, 64), :] = high
    dst[pl.ds(rows + 128, 64), :] = low


def kernel(
    q_hbm, k_hbm, v_hbm, w1_hbm, w2_hbm, gate_ref, out_ref,
    kv, qb, w1, w2, w2c, w1s, w2s, act, slope, ones,
    grad, other, chip_out, chips, plane_out, planes, part_out, part_in, total_out, total_in,
    cross_out, cross, centres, scores, att, tops, totals, sums,
    local_sem, load_sem, a2a_send, a2a_recv, q_send, q_recv, ring_send, ring_recv, core_send, core_recv,
    g_send, g_recv, chip_send, chip_recv, plane_send, plane_recv, back_send, back_recv,
    cross_send, cross_recv,
):
    seg = lax.axis_index("seg")
    y = lax.axis_index("head")
    z = seg // 8
    s = seg % 8
    x = s // 2
    c = s % 2

    def at(zz, xx, cc, yy):
        return {"seg": zz * 8 + xx * 2 + cc, "head": yy}

    def x_peer(d):
        return at(z, (x + d) % NX, c, y)

    twin = at(z, x, 1 - c, y)

    def send(src, dst, send_sem, recv_sem, device):
        copy = pltpu.make_async_remote_copy(
            src_ref=src, dst_ref=dst, send_sem=send_sem, recv_sem=recv_sem, device_id=device, device_id_type=MESH
        )
        copy.start()
        return copy

    def wait(copies):
        for copy in copies:
            copy.wait()

    barrier = pltpu.get_barrier_semaphore()
    peers = [at((z + d) % NZ, x, c, y) for d in range(1, NZ)]
    peers += [at(z, x, c, (y + d) % NY) for d in range(1, NY)]
    peers += [x_peer(d) for d in range(1, NX)]
    peers += [twin]
    for peer in peers:
        pl.semaphore_signal(barrier, inc=1, device_id=peer, device_id_type=MESH)

    load1 = pltpu.make_async_copy(w1_hbm, w1, load_sem.at[0])
    load2 = pltpu.make_async_copy(w2_hbm, w2, load_sem.at[1])
    load1.start()
    load2.start()

    def part(yy, p):
        return pl.ds(pl.multiple_of(yy * WIDTH + p * 128, 128), 128)

    rows_of_y = pl.ds(pl.multiple_of(y * 64, 64), 64)
    sources = (k_hbm, v_hbm)
    own_tokens = [[], [], []]
    for p in range(PAIRS):
        for t in range(2):
            copy = pltpu.make_async_copy(
                sources[t].at[:, part(y, p)], kv.at[p, s, t, rows_of_y], local_sem.at[p, t]
            )
            copy.start()
            own_tokens[p].append(copy)
    own_query = []
    for p in range(PAIRS):
        copy = pltpu.make_async_copy(q_hbm.at[:, part(y, p)], qb.at[p, rows_of_y], local_sem.at[p, 2])
        copy.start()
        own_query.append(copy)

    w1s[...] = jnp.zeros_like(w1s)
    w2s[...] = jnp.zeros_like(w2s)
    row = lax.broadcasted_iota(jnp.int32, (256, 128), 0)
    col = lax.broadcasted_iota(jnp.int32, (256, 128), 1)
    ones[...] = jnp.where((row % 128) // 64 == col // 64, 1.0 / 64, 0.0).astype(BF16)
    load1.wait()
    load2.wait()
    for h in range(HEADS):
        put_weights(w1s.at[0, h], h % 2 * 64, w1[h])
        centred = w2[h] - jnp.mean(w2[h], axis=0, keepdims=True)
        w2c[h] = centred
        put_weights(w2s.at[0, h], h % 2 * 64, centred)

    pl.semaphore_wait(barrier, len(peers))

    tokens = [[], [], []]
    for p in range(PAIRS):
        for d in (2, 1, 3):
            yy = (y + d) % NY
            for t in range(2):
                tokens[p].append(
                    send(
                        sources[t].at[:, part(yy, p)], kv.at[p, s, t, rows_of_y],
                        a2a_send.at[p, t, d], a2a_recv.at[p, t, d], at(z, x, c, yy),
                    )
                )
    query_copies = []
    for p in range(PAIRS):
        for d in (2, 1, 3):
            yy = (y + d) % NY
            query_copies.append(
                send(
                    q_hbm.at[:, part(yy, p)], qb.at[p, rows_of_y], q_send.at[p, d], q_recv.at[p, d],
                    at(z, x, c, yy),
                )
            )

    def gradients(p):
        keys = kv[p, s, 0]
        doubled = jnp.concatenate([keys, keys], axis=1)
        centre = jnp.zeros((ROWS, 128), F32)
        for half in range(2):
            h = 2 * p + half
            hidden = nn(doubled, w1s[0, h])
            square = hidden * hidden
            bent = jnp.tanh(hidden * (GELU_A + GELU_A * GELU_B * square))
            rise = 0.5 + 0.5 * bent
            act[half] = (hidden * rise).astype(BF16)
            slope[half] = rise + 0.5 * hidden * (1.0 - bent * bent) * (GELU_A + 3 * GELU_A * GELU_B * square)
            u = nt(act[half], w2s[0, h])
            centre = centre + u[:, :128] + u[:, 128:]
        inverse = lax.rsqrt(half_mean(centre * centre, ones[...]) + EPS)
        normal = centre * inverse
        target = kv[p, s, 1].astype(F32) - keys.astype(F32)
        error = (normal - target) * (1.0 / ROWS)
        du = inverse * (error - half_mean(error, ones[...]) - normal * half_mean(error * normal, ones[...]))
        high, low = split(du)
        both = jnp.concatenate([high, low], axis=1)
        twice = jnp.concatenate([high, high], axis=1)
        for half in range(2):
            second = tn(both, act[half])
            second = second[half * 64 : half * 64 + 64] + second[128 + half * 64 : 128 + half * 64 + 64]
            dh = (nn(twice, w2s[0, 2 * p + half]) * slope[half]).astype(BF16)
            grad[p, half, :64] = tn(keys, dh)[half * 64 : half * 64 + 64]
            grad[p, half, 64:] = second

    def to_other_core(p):
        return send(grad.at[p, 1 - c], other.at[p], g_send.at[p], g_recv.at[p], twin)

    def along_x(p):
        chip_out[p] = (grad[p, c] + other[p]).astype(CHIP_T).reshape(NX, PIECE, 256)
        copies = [
            send(chip_out.at[p, (x + d) % NX], chips.at[p, x], chip_send.at[p, d], chip_recv.at[p, d], x_peer(d))
            for d in (2, 1, 3)
        ]
        chips[p, x] = chip_out[p, x]
        return copies

    def along_z(p):
        plane = chips[p, 0].astype(F32)
        for k in range(1, NX):
            plane = plane + chips[p, k].astype(F32)
        plane_out[p] = plane.astype(PLANE_T)
        return [
            send(
                plane_out.at[p], planes.at[p, z], plane_send.at[p, d], plane_recv.at[p, d],
                at((z + d) % NZ, x, c, y),
            )
            for d in (4, 3, 5, 2, 6, 1, 7)
        ]

    low_plane = z < NZ // 2

    def back_along_x(p):
        low_sum = jnp.zeros((PIECE, 256), F32)
        high_sum = jnp.zeros((PIECE, 256), F32)
        for d in range(1, NZ):
            zz = (z + d) % NZ
            value = planes[p, zz].astype(F32)
            low_sum = low_sum + jnp.where(zz < z, value, 0.0)
            high_sum = high_sum + jnp.where(zz > z, value, 0.0)
        ahead_of = []
        run = low_sum
        for k in range(NX):
            ahead_of.append(run)
            run = run + chips[p, k].astype(F32)
        total_out[p] = run + high_sum
        run = high_sum
        for k in reversed(range(NX)):
            part_out[p, k] = jnp.where(low_plane, ahead_of[k], run).astype(BF16)
            run = run + chips[p, k].astype(F32)
        copies = []
        for d in (2, 1, 3):
            to = x_peer(d)
            copies.append(
                send(part_out.at[p, (x + d) % NX], part_in.at[p, x], back_send.at[p, 0, d], back_recv.at[p, 0, d], to)
            )
            copies.append(
                send(total_out.at[p], total_in.at[p, x], back_send.at[p, 1, d], back_recv.at[p, 1, d], to)
            )
        part_in[p, x] = part_out[p, x]
        total_in[p, x] = total_out[p]
        return copies

    is_one = c.astype(F32)
    is_zero = 1.0 - is_one

    def around(p):
        near = part_in[p].reshape(BLOCK, 256).astype(F32)
        rest = total_in[p].reshape(BLOCK, 256) - chip_out[p].reshape(BLOCK, 256).astype(F32) - near
        return jnp.where(low_plane, near, rest), jnp.where(low_plane, rest, near)

    def to_twin(p):
        own, oth = grad[p, c], other[p]
        ahead, behind = around(p)
        cross_out[p, 0] = ahead + oth + is_zero * own
        cross_out[p, 1] = behind + oth + is_one * own
        return [send(cross_out.at[p], cross.at[p], cross_send.at[p], cross_recv.at[p], twin)]

    def inner(p, half, side, value):
        h = 2 * p + half
        rows = pl.multiple_of(half * 64, 64)
        put_weights(w1s.at[side, h], rows, w1[h] - RATE * value[:64])
        put_weights(w2s.at[side, h], rows, w2c[h] - RATE * value[64:])
        query = qb[p]
        hidden = nn(jnp.concatenate([query, query], axis=1), w1s[side, h])
        bent = jnp.tanh(hidden * (GELU_A + GELU_A * GELU_B * hidden * hidden))
        high, low = split(hidden * (0.5 + 0.5 * bent))
        u = nt(high, w2s[side, h])
        return u[:, :128] + u[:, 128:] + nt(low, w2s[side, h, :128, :])

    def own_inner(p):
        own, oth = grad[p, c], other[p]
        ahead, behind = around(p)
        centres[p, 0] = inner(p, c, 0, ahead + own + is_one * oth)
        centres[p, 1] = inner(p, c, 1, behind + own + is_zero * oth)

    def finish(p):
        query = qb[p].astype(F32)
        result = att[p]
        for side in range(2):
            centre = centres[p, side] + inner(p, 1 - c, side, cross[p, side])
            inverse = lax.rsqrt(half_mean(centre * centre, ones[...]) + EPS)
            gate = jnp.tanh(gate_ref[side : side + 1, p * 128 : p * 128 + 128])
            result = result + gate * (query + centre * inverse)
        out_ref[:, p * 128 : p * 128 + 128] = result

    left, right, far = (s + 6) % 8, (s + 2) % 8, (s + 4) % 8
    given = [[], [], []]

    def twin_slot(slot):
        return slot + 1 - 2 * c

    def give(p, slot, k):
        given[p].append(send(kv.at[p, slot], kv.at[p, slot], core_send.at[p, k], core_recv.at[p, k], twin))

    def first_hop(p):
        give(p, s, 0)
        return [
            send(kv.at[p, s], kv.at[p, s], ring_send.at[p, k], ring_recv.at[p, k], x_peer(d))
            for k, d in enumerate((1, NX - 1))
        ]

    def second_hop(p):
        copies = [
            send(kv.at[p, slot, t], kv.at[p, slot, t], ring_send.at[p, 2 + t], ring_recv.at[p, 2 + t], x_peer(d))
            for t, (slot, d) in enumerate(((left, 1), (right, NX - 1)))
        ]
        give(p, left, 1)
        give(p, right, 2)
        return copies

    lane = lax.broadcasted_iota(jnp.int32, (ROWS, 128), 1)

    near_slots = (s, twin_slot(s), left, twin_slot(left), right, twin_slot(right))
    far_slots = (far, twin_slot(far))

    def attend_half(p, half, slots, last):
        pair = qb[p]
        index = 2 * p + half
        query = jnp.where(lane // 64 == half, pair, jnp.zeros_like(pair))
        top = tops[index] if last else None
        for k, slot in enumerate(slots):
            block = nt(query, kv[p, slot, 0])
            scores[k] = block
            peak = jnp.maximum(block[:, :128], block[:, 128:])
            top = peak if top is None else jnp.maximum(top, peak)
        top = jnp.max(top, axis=1, keepdims=True)
        if last:
            fade = jnp.exp2((tops[index] - top) * SCALE)
            total, summed = totals[index] * fade, sums[index] * fade
        else:
            total = jnp.zeros((ROWS, 128), F32)
            summed = jnp.zeros((ROWS, 128), F32)
        for k, slot in enumerate(slots):
            weight = jnp.exp2((scores[k] - top) * SCALE)
            total = total + weight[:, :128] + weight[:, 128:]
            summed = summed + nn(weight.astype(BF16), kv[p, slot, 1])
        if last:
            summed = summed / jnp.sum(total, axis=1, keepdims=True)
            att[p] = summed if half == 0 else jnp.where(lane < 64, att[p], summed)
        else:
            tops[index] = jnp.broadcast_to(top, (ROWS, 128))
            totals[index] = total
            sums[index] = summed

    def attend_near(p, half):
        attend_half(p, half, near_slots, False)

    def attend_far(p):
        for half in range(2):
            attend_half(p, half, far_slots, True)

    wait(own_tokens[0] + tokens[0])
    hop0 = first_hop(0)
    gradients(0)
    swap0 = to_other_core(0)
    wait(own_tokens[1] + tokens[1])
    hop1 = first_hop(1)
    gradients(1)
    swap1 = to_other_core(1)
    swap0.wait()
    chip0 = along_x(0)
    wait(own_tokens[2] + tokens[2])
    hop2 = first_hop(2)
    gradients(2)
    swap2 = to_other_core(2)
    swap1.wait()
    chip1 = along_x(1)
    swap2.wait()
    chip2 = along_x(2)
    wait(hop0)
    more0 = second_hop(0)
    wait(hop1)
    more1 = second_hop(1)
    wait(chip0)
    plane0 = along_z(0)
    wait(chip1)
    plane1 = along_z(1)
    wait(chip2)
    plane2 = along_z(2)
    wait(hop2)
    more2 = second_hop(2)
    wait(own_query + query_copies)
    wait(given[0])
    attend_near(0, 0)
    attend_near(0, 1)
    wait(plane0)
    back0 = back_along_x(0)
    wait(given[1])
    attend_near(1, 0)
    wait(plane1)
    back1 = back_along_x(1)
    attend_near(1, 1)
    wait(more0)
    give(0, far, 3)
    wait(given[2])
    attend_near(2, 0)
    wait(plane2)
    back2 = back_along_x(2)
    wait(more1)
    give(1, far, 3)
    attend_near(2, 1)
    wait(more2)
    give(2, far, 3)
    wait(back0)
    cross0 = to_twin(0)
    wait(given[0][3:])
    attend_far(0)
    own_inner(0)
    wait(back1)
    cross1 = to_twin(1)
    wait(given[1][3:])
    attend_far(1)
    own_inner(1)
    wait(given[2][3:])
    attend_far(2)
    wait(cross0)
    finish(0)
    wait(back2)
    cross2 = to_twin(2)
    own_inner(2)
    wait(cross1)
    finish(1)
    wait(cross2)
    finish(2)


def on_device(queries, key_rows, value_rows, w_first, w_second, gate_pairs):
    dma = pltpu.SemaphoreType.DMA
    hbm = pl.BlockSpec(memory_space=pl.ANY)
    vmem = pl.BlockSpec(memory_space=pltpu.VMEM)
    scratch = [
        pltpu.VMEM((PAIRS, 8, 2, ROWS, 128), BF16),
        pltpu.VMEM((PAIRS, ROWS, 128), BF16),
        pltpu.VMEM((HEADS, 64, 256), F32),
        pltpu.VMEM((HEADS, 64, 256), F32),
        pltpu.VMEM((HEADS, 64, 256), F32),
        pltpu.VMEM((2, HEADS, 256, 256), BF16),
        pltpu.VMEM((2, HEADS, 256, 256), BF16),
        pltpu.VMEM((2, ROWS, 256), BF16),
        pltpu.VMEM((2, ROWS, 256), F32),
        pltpu.VMEM((256, 128), BF16),
        pltpu.VMEM((PAIRS, 2, BLOCK, 256), F32),
        pltpu.VMEM((PAIRS, BLOCK, 256), F32),
        pltpu.VMEM((PAIRS, NX, PIECE, 256), CHIP_T),
        pltpu.VMEM((PAIRS, NX, PIECE, 256), CHIP_T),
        pltpu.VMEM((PAIRS, PIECE, 256), PLANE_T),
        pltpu.VMEM((PAIRS, NZ, PIECE, 256), PLANE_T),
        pltpu.VMEM((PAIRS, NX, PIECE, 256), BF16),
        pltpu.VMEM((PAIRS, NX, PIECE, 256), BF16),
        pltpu.VMEM((PAIRS, PIECE, 256), F32),
        pltpu.VMEM((PAIRS, NX, PIECE, 256), F32),
        pltpu.VMEM((PAIRS, 2, BLOCK, 256), F32),
        pltpu.VMEM((PAIRS, 2, BLOCK, 256), F32),
        pltpu.VMEM((PAIRS, 2, ROWS, 128), F32),
        pltpu.VMEM((6, ROWS, 256), F32),
        pltpu.VMEM((PAIRS, ROWS, 128), F32),
        pltpu.VMEM((HEADS, ROWS, 128), F32),
        pltpu.VMEM((HEADS, ROWS, 128), F32),
        pltpu.VMEM((HEADS, ROWS, 128), F32),
        dma((PAIRS, 3)),
        dma((2,)),
        dma((PAIRS, 2, NY)),
        dma((PAIRS, 2, NY)),
        dma((PAIRS, NY)),
        dma((PAIRS, NY)),
        dma((PAIRS, 4)),
        dma((PAIRS, 4)),
        dma((PAIRS, 4)),
        dma((PAIRS, 4)),
        dma((PAIRS,)),
        dma((PAIRS,)),
        dma((PAIRS, NX)),
        dma((PAIRS, NX)),
        dma((PAIRS, NZ)),
        dma((PAIRS, NZ)),
        dma((PAIRS, 2, NX)),
        dma((PAIRS, 2, NX)),
        dma((PAIRS,)),
        dma((PAIRS,)),
    ]
    return pl.pallas_call(
        kernel,
        out_shape=jax.ShapeDtypeStruct((ROWS, WIDTH), F32),
        in_specs=[hbm, hbm, hbm, hbm, hbm, vmem],
        out_specs=vmem,
        scratch_shapes=scratch,
        compiler_params=pltpu.CompilerParams(
            collective_id=0, has_side_effects=True, vmem_limit_bytes=62 * 1024 * 1024
        ),
        name="layer",
    )(queries, key_rows, value_rows, w_first, jnp.swapaxes(w_second, 1, 2), gate_pairs)


def solution(mesh):
    in_specs = (
        P(("seg", "head"), None),
        P(("seg", "head"), None),
        P(("seg", "head"), None),
        P("head", None, None),
        P("head", None, None),
        P(None, "head"),
    )
    out_specs = P("seg", "head")
    return jax.shard_map(on_device, mesh=mesh, in_specs=in_specs, out_specs=out_specs, check_vma=False)
```

```python
import jax
import jax.numpy as jnp
from jax import lax
from jax.experimental import pallas as pl
from jax.experimental.pallas import tpu as pltpu
from jax.sharding import PartitionSpec as P

MESH = pl.DeviceIdType.MESH
F32 = jnp.float32
BF16 = jnp.bfloat16

NX, NC, NY, NZ = 4, 2, 4, 8
HEADS = 6
PAIRS = 3
ROWS = 256
WIDTH = 384
BLOCK = 128
PIECE = BLOCK // NX
RATE = 0.05
EPS = 1e-5
SCALE = 0.125 * 1.4426950408889634

CHIP_T = BF16
PLANE_T = BF16


def nn(a, b):
    return lax.dot_general(a, b, (((1,), (0,)), ((), ())), preferred_element_type=F32)


def nt(a, b):
    return lax.dot_general(a, b, (((1,), (1,)), ((), ())), preferred_element_type=F32)


def tn(a, b):
    return lax.dot_general(a, b, (((0,), (0,)), ((), ())), preferred_element_type=F32)


def split(x):
    high = x.astype(BF16)
    return high, (x - high.astype(F32)).astype(BF16)


def half_mean(x, ones):
    high, low = split(x)
    return nn(jnp.concatenate([high, low], axis=1), ones)


GELU_A = 0.7978845608028654
GELU_B = 0.044715


def put_weights(dst, rows, value):
    high, low = split(value)
    dst[pl.ds(rows, 64), :] = high
    dst[pl.ds(rows + 128, 64), :] = low


def kernel(
    q_hbm, k_hbm, v_hbm, w1_hbm, w2_hbm, gate_ref, out_ref,
    kv, qb, w1, w2, w2c, w1s, w2s, act, slope, ones,
    grad, other, chip_out, chips, plane_out, planes, part_out, part_in, total_out, total_in,
    cross_out, cross, centres, scores, att, tops, totals, sums,
    local_sem, load_sem, a2a_send, a2a_recv, q_send, q_recv, ring_send, ring_recv, core_send, core_recv,
    g_send, g_recv, chip_send, chip_recv, plane_send, plane_recv, back_send, back_recv,
    cross_send, cross_recv,
):
    seg = lax.axis_index("seg")
    y = lax.axis_index("head")
    z = seg // 8
    s = seg % 8
    x = s // 2
    c = s % 2

    def at(zz, xx, cc, yy):
        return {"seg": zz * 8 + xx * 2 + cc, "head": yy}

    def x_peer(d):
        return at(z, (x + d) % NX, c, y)

    twin = at(z, x, 1 - c, y)

    def send(src, dst, send_sem, recv_sem, device):
        copy = pltpu.make_async_remote_copy(
            src_ref=src, dst_ref=dst, send_sem=send_sem, recv_sem=recv_sem, device_id=device, device_id_type=MESH
        )
        copy.start()
        return copy

    def wait(copies):
        for copy in copies:
            copy.wait()

    barrier = pltpu.get_barrier_semaphore()
    peers = [at((z + d) % NZ, x, c, y) for d in range(1, NZ)]
    peers += [at(z, x, c, (y + d) % NY) for d in range(1, NY)]
    peers += [x_peer(d) for d in range(1, NX)]
    peers += [twin]
    for peer in peers:
        pl.semaphore_signal(barrier, inc=1, device_id=peer, device_id_type=MESH)

    load1 = pltpu.make_async_copy(w1_hbm, w1, load_sem.at[0])
    load2 = pltpu.make_async_copy(w2_hbm, w2, load_sem.at[1])
    load1.start()
    load2.start()

    def part(yy, p):
        return pl.ds(pl.multiple_of(yy * WIDTH + p * 128, 128), 128)

    rows_of_y = pl.ds(pl.multiple_of(y * 64, 64), 64)
    sources = (k_hbm, v_hbm)
    own_tokens = [[], [], []]
    for p in range(PAIRS):
        for t in range(2):
            copy = pltpu.make_async_copy(
                sources[t].at[:, part(y, p)], kv.at[p, s, t, rows_of_y], local_sem.at[p, t]
            )
            copy.start()
            own_tokens[p].append(copy)
    own_query = []
    for p in range(PAIRS):
        copy = pltpu.make_async_copy(q_hbm.at[:, part(y, p)], qb.at[p, rows_of_y], local_sem.at[p, 2])
        copy.start()
        own_query.append(copy)

    w1s[...] = jnp.zeros_like(w1s)
    w2s[...] = jnp.zeros_like(w2s)
    row = lax.broadcasted_iota(jnp.int32, (256, 128), 0)
    col = lax.broadcasted_iota(jnp.int32, (256, 128), 1)
    ones[...] = jnp.where((row % 128) // 64 == col // 64, 1.0 / 64, 0.0).astype(BF16)
    load1.wait()
    load2.wait()
    for h in range(HEADS):
        put_weights(w1s.at[0, h], h % 2 * 64, w1[h])
        centred = w2[h] - jnp.mean(w2[h], axis=0, keepdims=True)
        w2c[h] = centred
        put_weights(w2s.at[0, h], h % 2 * 64, centred)

    pl.semaphore_wait(barrier, len(peers))

    tokens = [[], [], []]
    for p in range(PAIRS):
        for d in (2, 1, 3):
            yy = (y + d) % NY
            for t in range(2):
                tokens[p].append(
                    send(
                        sources[t].at[:, part(yy, p)], kv.at[p, s, t, rows_of_y],
                        a2a_send.at[p, t, d], a2a_recv.at[p, t, d], at(z, x, c, yy),
                    )
                )
    query_copies = []
    for p in range(PAIRS):
        for d in (2, 1, 3):
            yy = (y + d) % NY
            query_copies.append(
                send(
                    q_hbm.at[:, part(yy, p)], qb.at[p, rows_of_y], q_send.at[p, d], q_recv.at[p, d],
                    at(z, x, c, yy),
                )
            )

    def gradients(p):
        keys = kv[p, s, 0]
        doubled = jnp.concatenate([keys, keys], axis=1)
        centre = jnp.zeros((ROWS, 128), F32)
        for half in range(2):
            h = 2 * p + half
            hidden = nn(doubled, w1s[0, h])
            square = hidden * hidden
            bent = jnp.tanh(hidden * (GELU_A + GELU_A * GELU_B * square))
            rise = 0.5 + 0.5 * bent
            act[half] = (hidden * rise).astype(BF16)
            slope[half] = rise + 0.5 * hidden * (1.0 - bent * bent) * (GELU_A + 3 * GELU_A * GELU_B * square)
            u = nt(act[half], w2s[0, h])
            centre = centre + u[:, :128] + u[:, 128:]
        inverse = lax.rsqrt(half_mean(centre * centre, ones[...]) + EPS)
        normal = centre * inverse
        target = kv[p, s, 1].astype(F32) - keys.astype(F32)
        error = (normal - target) * (1.0 / ROWS)
        du = inverse * (error - half_mean(error, ones[...]) - normal * half_mean(error * normal, ones[...]))
        high, low = split(du)
        both = jnp.concatenate([high, low], axis=1)
        twice = jnp.concatenate([high, high], axis=1)
        for half in range(2):
            second = tn(both, act[half])
            second = second[half * 64 : half * 64 + 64] + second[128 + half * 64 : 128 + half * 64 + 64]
            dh = (nn(twice, w2s[0, 2 * p + half]) * slope[half]).astype(BF16)
            grad[p, half, :64] = tn(keys, dh)[half * 64 : half * 64 + 64]
            grad[p, half, 64:] = second

    def to_other_core(p):
        return send(grad.at[p, 1 - c], other.at[p], g_send.at[p], g_recv.at[p], twin)

    def along_x(p):
        chip_out[p] = (grad[p, c] + other[p]).astype(CHIP_T).reshape(NX, PIECE, 256)
        copies = [
            send(chip_out.at[p, (x + d) % NX], chips.at[p, x], chip_send.at[p, d], chip_recv.at[p, d], x_peer(d))
            for d in (2, 1, 3)
        ]
        chips[p, x] = chip_out[p, x]
        return copies

    def along_z(p):
        plane = chips[p, 0].astype(F32)
        for k in range(1, NX):
            plane = plane + chips[p, k].astype(F32)
        plane_out[p] = plane.astype(PLANE_T)
        return [
            send(
                plane_out.at[p], planes.at[p, z], plane_send.at[p, d], plane_recv.at[p, d],
                at((z + d) % NZ, x, c, y),
            )
            for d in (4, 3, 5, 2, 6, 1, 7)
        ]

    low_plane = z < NZ // 2

    def back_along_x(p):
        low_sum = jnp.zeros((PIECE, 256), F32)
        high_sum = jnp.zeros((PIECE, 256), F32)
        for d in range(1, NZ):
            zz = (z + d) % NZ
            value = planes[p, zz].astype(F32)
            low_sum = low_sum + jnp.where(zz < z, value, 0.0)
            high_sum = high_sum + jnp.where(zz > z, value, 0.0)
        ahead_of = []
        run = low_sum
        for k in range(NX):
            ahead_of.append(run)
            run = run + chips[p, k].astype(F32)
        total_out[p] = run + high_sum
        run = high_sum
        for k in reversed(range(NX)):
            part_out[p, k] = jnp.where(low_plane, ahead_of[k], run).astype(BF16)
            run = run + chips[p, k].astype(F32)
        copies = []
        for d in (2, 1, 3):
            to = x_peer(d)
            copies.append(
                send(part_out.at[p, (x + d) % NX], part_in.at[p, x], back_send.at[p, 0, d], back_recv.at[p, 0, d], to)
            )
            copies.append(
                send(total_out.at[p], total_in.at[p, x], back_send.at[p, 1, d], back_recv.at[p, 1, d], to)
            )
        part_in[p, x] = part_out[p, x]
        total_in[p, x] = total_out[p]
        return copies

    is_one = c.astype(F32)
    is_zero = 1.0 - is_one

    def around(p):
        near = part_in[p].reshape(BLOCK, 256).astype(F32)
        rest = total_in[p].reshape(BLOCK, 256) - chip_out[p].reshape(BLOCK, 256).astype(F32) - near
        return jnp.where(low_plane, near, rest), jnp.where(low_plane, rest, near)

    def to_twin(p):
        own, oth = grad[p, c], other[p]
        ahead, behind = around(p)
        cross_out[p, 0] = ahead + oth + is_zero * own
        cross_out[p, 1] = behind + oth + is_one * own
        return [send(cross_out.at[p], cross.at[p], cross_send.at[p], cross_recv.at[p], twin)]

    def inner(p, half, side, value):
        h = 2 * p + half
        rows = pl.multiple_of(half * 64, 64)
        put_weights(w1s.at[side, h], rows, w1[h] - RATE * value[:64])
        put_weights(w2s.at[side, h], rows, w2c[h] - RATE * value[64:])
        query = qb[p]
        hidden = nn(jnp.concatenate([query, query], axis=1), w1s[side, h])
        bent = jnp.tanh(hidden * (GELU_A + GELU_A * GELU_B * hidden * hidden))
        high, low = split(hidden * (0.5 + 0.5 * bent))
        u = nt(high, w2s[side, h])
        return u[:, :128] + u[:, 128:] + nt(low, w2s[side, h, :128, :])

    def own_inner(p):
        own, oth = grad[p, c], other[p]
        ahead, behind = around(p)
        centres[p, 0] = inner(p, c, 0, ahead + own + is_one * oth)
        centres[p, 1] = inner(p, c, 1, behind + own + is_zero * oth)

    def finish(p):
        query = qb[p].astype(F32)
        result = att[p]
        for side in range(2):
            centre = centres[p, side] + inner(p, 1 - c, side, cross[p, side])
            inverse = lax.rsqrt(half_mean(centre * centre, ones[...]) + EPS)
            gate = jnp.tanh(gate_ref[side : side + 1, p * 128 : p * 128 + 128])
            result = result + gate * (query + centre * inverse)
        out_ref[:, p * 128 : p * 128 + 128] = result

    left, right, far = (s + 6) % 8, (s + 2) % 8, (s + 4) % 8
    given = [[], [], []]

    def twin_slot(slot):
        return slot + 1 - 2 * c

    def give(p, slot, k):
        given[p].append(send(kv.at[p, slot], kv.at[p, slot], core_send.at[p, k], core_recv.at[p, k], twin))

    def first_hop(p):
        give(p, s, 0)
        return [
            send(kv.at[p, s], kv.at[p, s], ring_send.at[p, k], ring_recv.at[p, k], x_peer(d))
            for k, d in enumerate((1, NX - 1))
        ]

    def second_hop(p):
        copies = [
            send(kv.at[p, slot, t], kv.at[p, slot, t], ring_send.at[p, 2 + t], ring_recv.at[p, 2 + t], x_peer(d))
            for t, (slot, d) in enumerate(((left, 1), (right, NX - 1)))
        ]
        give(p, left, 1)
        give(p, right, 2)
        return copies

    lane = lax.broadcasted_iota(jnp.int32, (ROWS, 128), 1)

    near_slots = (s, twin_slot(s), left, twin_slot(left), right, twin_slot(right))
    far_slots = (far, twin_slot(far))

    def attend_half(p, half, slots, last):
        pair = qb[p]
        index = 2 * p + half
        query = jnp.where(lane // 64 == half, pair, jnp.zeros_like(pair))
        top = tops[index] if last else None
        for k, slot in enumerate(slots):
            block = nt(query, kv[p, slot, 0])
            scores[k] = block
            peak = jnp.maximum(block[:, :128], block[:, 128:])
            top = peak if top is None else jnp.maximum(top, peak)
        top = jnp.max(top, axis=1, keepdims=True)
        if last:
            fade = jnp.exp2((tops[index] - top) * SCALE)
            total, summed = totals[index] * fade, sums[index] * fade
        else:
            total = jnp.zeros((ROWS, 128), F32)
            summed = jnp.zeros((ROWS, 128), F32)
        for k, slot in enumerate(slots):
            weight = jnp.exp2((scores[k] - top) * SCALE)
            total = total + weight[:, :128] + weight[:, 128:]
            summed = summed + nn(weight.astype(BF16), kv[p, slot, 1])
        if last:
            summed = summed / jnp.sum(total, axis=1, keepdims=True)
            att[p] = summed if half == 0 else jnp.where(lane < 64, att[p], summed)
        else:
            tops[index] = jnp.broadcast_to(top, (ROWS, 128))
            totals[index] = total
            sums[index] = summed

    def attend_near(p, half):
        attend_half(p, half, near_slots, False)

    def attend_far(p):
        for half in range(2):
            attend_half(p, half, far_slots, True)

    wait(own_tokens[0] + tokens[0])
    hop0 = first_hop(0)
    gradients(0)
    swap0 = to_other_core(0)
    wait(own_tokens[1] + tokens[1])
    hop1 = first_hop(1)
    gradients(1)
    swap1 = to_other_core(1)
    swap0.wait()
    chip0 = along_x(0)
    wait(own_tokens[2] + tokens[2])
    hop2 = first_hop(2)
    gradients(2)
    swap2 = to_other_core(2)
    swap1.wait()
    chip1 = along_x(1)
    swap2.wait()
    chip2 = along_x(2)
    wait(hop0)
    more0 = second_hop(0)
    wait(hop1)
    more1 = second_hop(1)
    wait(chip0)
    plane0 = along_z(0)
    wait(chip1)
    plane1 = along_z(1)
    wait(chip2)
    plane2 = along_z(2)
    wait(hop2)
    more2 = second_hop(2)
    wait(own_query + query_copies)
    wait(given[0])
    attend_near(0, 0)
    attend_near(0, 1)
    wait(plane0)
    back0 = back_along_x(0)
    wait(given[1])
    attend_near(1, 0)
    wait(plane1)
    back1 = back_along_x(1)
    attend_near(1, 1)
    wait(more0)
    give(0, far, 3)
    wait(given[2])
    attend_near(2, 0)
    wait(plane2)
    back2 = back_along_x(2)
    wait(more1)
    give(1, far, 3)
    attend_near(2, 1)
    wait(given[0][3:])
    attend_far(0)
    wait(back0)
    cross0 = to_twin(0)
    wait(more2)
    give(2, far, 3)
    own_inner(0)
    wait(back1)
    cross1 = to_twin(1)
    wait(given[1][3:])
    attend_far(1)
    own_inner(1)
    wait(given[2][3:])
    attend_far(2)
    wait(cross0)
    finish(0)
    wait(back2)
    cross2 = to_twin(2)
    own_inner(2)
    wait(cross1)
    finish(1)
    wait(cross2)
    finish(2)


def on_device(queries, key_rows, value_rows, w_first, w_second, gate_pairs):
    dma = pltpu.SemaphoreType.DMA
    hbm = pl.BlockSpec(memory_space=pl.ANY)
    vmem = pl.BlockSpec(memory_space=pltpu.VMEM)
    scratch = [
        pltpu.VMEM((PAIRS, 8, 2, ROWS, 128), BF16),
        pltpu.VMEM((PAIRS, ROWS, 128), BF16),
        pltpu.VMEM((HEADS, 64, 256), F32),
        pltpu.VMEM((HEADS, 64, 256), F32),
        pltpu.VMEM((HEADS, 64, 256), F32),
        pltpu.VMEM((2, HEADS, 256, 256), BF16),
        pltpu.VMEM((2, HEADS, 256, 256), BF16),
        pltpu.VMEM((2, ROWS, 256), BF16),
        pltpu.VMEM((2, ROWS, 256), F32),
        pltpu.VMEM((256, 128), BF16),
        pltpu.VMEM((PAIRS, 2, BLOCK, 256), F32),
        pltpu.VMEM((PAIRS, BLOCK, 256), F32),
        pltpu.VMEM((PAIRS, NX, PIECE, 256), CHIP_T),
        pltpu.VMEM((PAIRS, NX, PIECE, 256), CHIP_T),
        pltpu.VMEM((PAIRS, PIECE, 256), PLANE_T),
        pltpu.VMEM((PAIRS, NZ, PIECE, 256), PLANE_T),
        pltpu.VMEM((PAIRS, NX, PIECE, 256), BF16),
        pltpu.VMEM((PAIRS, NX, PIECE, 256), BF16),
        pltpu.VMEM((PAIRS, PIECE, 256), F32),
        pltpu.VMEM((PAIRS, NX, PIECE, 256), F32),
        pltpu.VMEM((PAIRS, 2, BLOCK, 256), F32),
        pltpu.VMEM((PAIRS, 2, BLOCK, 256), F32),
        pltpu.VMEM((PAIRS, 2, ROWS, 128), F32),
        pltpu.VMEM((6, ROWS, 256), F32),
        pltpu.VMEM((PAIRS, ROWS, 128), F32),
        pltpu.VMEM((HEADS, ROWS, 128), F32),
        pltpu.VMEM((HEADS, ROWS, 128), F32),
        pltpu.VMEM((HEADS, ROWS, 128), F32),
        dma((PAIRS, 3)),
        dma((2,)),
        dma((PAIRS, 2, NY)),
        dma((PAIRS, 2, NY)),
        dma((PAIRS, NY)),
        dma((PAIRS, NY)),
        dma((PAIRS, 4)),
        dma((PAIRS, 4)),
        dma((PAIRS, 4)),
        dma((PAIRS, 4)),
        dma((PAIRS,)),
        dma((PAIRS,)),
        dma((PAIRS, NX)),
        dma((PAIRS, NX)),
        dma((PAIRS, NZ)),
        dma((PAIRS, NZ)),
        dma((PAIRS, 2, NX)),
        dma((PAIRS, 2, NX)),
        dma((PAIRS,)),
        dma((PAIRS,)),
    ]
    return pl.pallas_call(
        kernel,
        out_shape=jax.ShapeDtypeStruct((ROWS, WIDTH), F32),
        in_specs=[hbm, hbm, hbm, hbm, hbm, vmem],
        out_specs=vmem,
        scratch_shapes=scratch,
        compiler_params=pltpu.CompilerParams(
            collective_id=0, has_side_effects=True, vmem_limit_bytes=62 * 1024 * 1024
        ),
        name="layer",
    )(queries, key_rows, value_rows, w_first, jnp.swapaxes(w_second, 1, 2), gate_pairs)


def solution(mesh):
    in_specs = (
        P(("seg", "head"), None),
        P(("seg", "head"), None),
        P(("seg", "head"), None),
        P("head", None, None),
        P("head", None, None),
        P(None, "head"),
    )
    out_specs = P("seg", "head")
    return jax.shard_map(on_device, mesh=mesh, in_specs=in_specs, out_specs=out_specs, check_vma=False)
```
